256 devices in a mesh: scene: 32 (over x, y, core), kd: 8 (over z).
Axes of the slice: x: 4, y: 4, z: 8, core: 2. Of those that a mesh axis runs over, the one named last changes fastest.
Arguments:
- features: bfloat16 [32, 32, 512, 128], P('scene', 'kd'), may hold values from -6 to 6
- send_faces: int32 [32, 8, 3, 1], P('scene', 'kd'), may hold values from 0 to 23, as said below
- face_source: int32 [32, 32, 6], P('scene', 'kd'), may hold values from 0 to 27, as said below
- cotangent: bfloat16 [32, 32, 64, 256], P('scene', 'kd'), may hold values from -12 to 12
- conv_one: bfloat16 [7, 128, 128], replicated, may hold values from -0.1875 to 0.1875
- down_weight: bfloat16 [1024, 256], replicated, may hold values from -0.1875 to 0.1875
- conv_two: bfloat16 [7, 256, 256], replicated, may hold values from -0.125 to 0.125
Outputs:
- encoded: bfloat16 [32, 32, 64, 256], P('scene', 'kd')
- grad_conv_one: float32 [7, 128, 128], replicated
- grad_down: float32 [1024, 256], replicated
- grad_conv_two: float32 [7, 256, 256], replicated
The draws below stay inside these ranges and needn't reach their ends.
Inputs may be any that keep to these rules, and one draw needn't show every extreme that they name: `send_faces`: entry [i, t] names face 6 b + s of the sender's own brick b; across bit i every device sends exactly one face, of side 2 (i mod 3) + 1 where its bit i is 0 and of side 2 (i mod 3) where it is 1; no face is named twice on a device. `face_source`: for brick b and direction s: a value under 6 * 4 is a local face, of the side opposite s; 24 + i + t is slot t received across bit i; 27 is no neighbour. The relation is symmetric: where direction s of brick b takes a face of brick b2, direction opposite s of b2 takes the face of b at side s, across devices through the same bit and slot.
All inputs are finite; a program needn't handle non-finite values.
Results may differ from the reference program's by a relative error of at most 0.0065.
Values may be sent and summed in bfloat16 or wider, within the bound.
No kernel may reach another device: no remote copies, remote signals or barrier semaphores. Data moves between devices by JAX's collectives and lax.ppermute only.
A program may use at most 64 MiB of HBM per device.

```python
import jax
import jax.numpy as jnp
from jax import lax

C1 = 128
C2 = 256
BRICKS = 4
SLOTS = 1
NBITS = 3
SCENES = 32
NB = 32
N_KD = 8


def brick_lists(key):
    empty_slot = 6 * BRICKS + NBITS * SLOTS

    def one_device(device_key, device):
        shuffled = jax.random.permutation(jax.random.fold_in(device_key, 1), BRICKS).astype(jnp.int32)
        source = jnp.full((BRICKS * 6,), empty_slot, jnp.int32)
        outgoing = []
        for bit_index in range(NBITS):
            axis_id = bit_index % 3
            upper_side = jnp.bitwise_and(jnp.right_shift(device, bit_index), 1)
            face_ids = shuffled[bit_index * SLOTS:(bit_index + 1) * SLOTS] * 6 + 2 * axis_id + 1 - upper_side
            outgoing.append(face_ids)
            source = source.at[face_ids].set(6 * BRICKS + bit_index * SLOTS + jnp.arange(SLOTS, dtype=jnp.int32))
        for axis_id in range(3):
            chain_order = jax.random.permutation(jax.random.fold_in(device_key, 10 + axis_id), BRICKS).astype(jnp.int32)
            keep_mask = jax.random.randint(jax.random.fold_in(device_key, 20 + axis_id), (BRICKS - 1,), 0, 4) > 0
            plus_ids = chain_order[:-1] * 6 + 2 * axis_id + 1
            minus_ids = chain_order[1:] * 6 + 2 * axis_id
            plus_old = source[plus_ids]
            minus_old = source[minus_ids]
            linked = keep_mask & (plus_old == empty_slot) & (minus_old == empty_slot)
            source = source.at[plus_ids].set(jnp.where(linked, minus_ids, plus_old))
            source = source.at[minus_ids].set(jnp.where(linked, plus_ids, minus_old))
        return (jnp.stack(outgoing), source.reshape(BRICKS, 6))

    def one_scene(scene):
        scene_key = jax.random.fold_in(jax.random.fold_in(key, 977), scene)
        return jax.vmap(lambda device: one_device(jax.random.fold_in(scene_key, device), device))(jnp.arange(N_KD, dtype=jnp.int32))
    outgoing, source = jax.vmap(one_scene)(jnp.arange(SCENES, dtype=jnp.int32))
    return (outgoing, source.reshape(SCENES, N_KD * BRICKS, 6))


def draw_send_faces(key, part):
    return brick_lists(key)[0]


def draw_face_source(key, part):
    return brick_lists(key)[1]


def spiked(entries, stream_key, source, target, parts, factor):
    def block_of(position):
        return (jnp.arange(entries.shape[position]) // (entries.shape[position] // parts)).reshape((-1,) + (1,) * (entries.ndim - 1 - position))

    one_side = jax.random.permutation(stream_key, parts)[block_of(target)]
    other_side = (block_of(target) + parts // 2) % parts
    return jnp.where((block_of(source) == one_side) | (block_of(source) == other_side), factor * entries, entries)


def level_of(rng, dims, pieces, smallest, high):
    gain, own = 1.0, jax.random.fold_in(rng, 6)
    for dim, shards_of in pieces:
        heights = jnp.exp(jax.random.uniform(jax.random.fold_in(own, dim), (shards_of,), jnp.float32, smallest / len(pieces), high / len(pieces)))
        gain = gain * jnp.repeat(heights, dims[dim] // shards_of).reshape([-1 if axis == dim else 1 for axis in range(len(dims))])
    return gain


def normal_values(key, shape, deviation, reach, split=(), kind=jnp.bfloat16):
    entries = deviation * jax.random.normal(key, shape, jnp.float32)
    if split:
        entries = entries * level_of(key, shape, split, -0.22, 0.18)
    return jnp.clip(entries, -reach, reach).astype(kind)


def noise_with(own_key, extent, width, most, pieces, heavy, kind=jnp.bfloat16):
    result = width * jax.random.normal(own_key, extent, jnp.float32)
    if pieces:
        result = result * level_of(own_key, extent, pieces, -0.22, 0.18)
    return jnp.clip(spiked(result, jax.random.fold_in(own_key, 3), *heavy), -most, most).astype(kind)


def setup_inputs(seed: int = 0) -> dict:
    keys = jax.random.split(jax.random.key(seed), 8)
    return {
        "features": normal_values(keys[0], (SCENES, NB, 512, C1), 1.0, 6.0, ((0, 32), (1, 8))),
        "send_faces": draw_send_faces(jax.random.fold_in(keys[7], 71), 0),
        "face_source": draw_face_source(jax.random.fold_in(keys[7], 71), 0),
        "cotangent": noise_with(keys[3], (SCENES, NB, 64, C2), 1.0, 12.0, ((0, 32), (1, 8)), (0, 3, 32, 2.75)),
        "conv_one": normal_values(keys[4], (7, C1, C1), (7 * C1) ** -0.5, 0.1875),
        "down_weight": normal_values(keys[5], (8 * C1, C2), (8 * C1) ** -0.5, 0.1875),
        "conv_two": normal_values(keys[6], (7, C2, C2), (7 * C2) ** -0.5, 0.125),
    }


OPPOSITE = (0, 2, 1, 4, 3, 6, 5)


def face_slabs(blocks):
    return jnp.stack([blocks[:, 0], blocks[:, -1], blocks[:, :, 0], blocks[:, :, -1], blocks[:, :, :, 0], blocks[:, :, :, -1]], axis=1)


def shift_taps(blocks, border):
    return [
        blocks,
        jnp.concatenate([border[:, 0][:, None], blocks[:, :-1]], 1),
        jnp.concatenate([blocks[:, 1:], border[:, 1][:, None]], 1),
        jnp.concatenate([border[:, 2][:, :, None], blocks[:, :, :-1]], 2),
        jnp.concatenate([blocks[:, :, 1:], border[:, 3][:, :, None]], 2),
        jnp.concatenate([border[:, 4][:, :, :, None], blocks[:, :, :, :-1]], 3),
        jnp.concatenate([blocks[:, :, :, 1:], border[:, 5][:, :, :, None]], 3),
    ]


def conv_apply(taps, weight):
    chans = taps[0].shape[-1]
    total = jnp.dot(taps[0].reshape(-1, chans), weight[0], preferred_element_type=jnp.float32)
    for tap_index in range(1, 7):
        total = total + jnp.dot(taps[tap_index].reshape(-1, chans), weight[tap_index], preferred_element_type=jnp.float32)
    return total


def conv_back(taps, weight):
    chans = taps[0].shape[-1]
    total = lax.dot_general(taps[0].reshape(-1, chans), weight[0], (((1,), (1,)), ((), ())), preferred_element_type=jnp.float32)
    for tap_index in range(1, 7):
        total = total + lax.dot_general(taps[OPPOSITE[tap_index]].reshape(-1, chans), weight[tap_index], (((1,), (1,)), ((), ())), preferred_element_type=jnp.float32)
    return total


def weight_grads(taps, delta):
    chans = taps[0].shape[-1]
    return jnp.stack([lax.dot_general(single.reshape(-1, chans), delta, (((0,), (0,)), ((), ())), preferred_element_type=jnp.float32) for single in taps])


def down_rows(hidden, brick_count, chans):
    return hidden.reshape(brick_count, 4, 2, 4, 2, 4, 2, chans).transpose(0, 1, 3, 5, 2, 4, 6, 7).reshape(brick_count * 64, 8 * chans)


def up_rows(patch_grad, brick_count, chans):
    return patch_grad.reshape(brick_count, 4, 4, 4, 2, 2, 2, chans).transpose(0, 1, 4, 2, 5, 3, 6, 7).reshape(brick_count * 512, chans)


def silu_slope(value):
    sigma = jax.nn.sigmoid(value)
    return sigma * (1.0 + value * (1.0 - sigma))


def scene_rims(blocks, scene_send, scene_source):
    devices = scene_send.shape[0]
    per_device = blocks.shape[0] // devices
    side_cells = blocks.shape[1]
    chans = blocks.shape[-1]
    faces = face_slabs(blocks).reshape(devices, per_device * 6, side_cells, side_cells, chans)
    outgoing = jax.vmap(lambda face_table, chosen: face_table[chosen])(faces, scene_send)
    device_ids = jnp.arange(devices, dtype=jnp.int32)
    incoming = jnp.stack([outgoing[jnp.bitwise_xor(device_ids, 1 << bit_index), bit_index] for bit_index in range(scene_send.shape[1])], axis=1)
    incoming = incoming.reshape(devices, -1, side_cells, side_cells, chans)
    empty = jnp.zeros((devices, 1, side_cells, side_cells, chans), blocks.dtype)
    lookup = jnp.concatenate([faces, incoming, empty], axis=1)
    border = jax.vmap(lambda device_table, chosen: device_table[chosen])(lookup, scene_source.reshape(devices, per_device, 6))
    return border.reshape(devices * per_device, 6, side_cells, side_cells, chans)


def reference(features, send_faces, face_source, cotangent, conv_one, down_weight, conv_two):
    def scene_pass(carry, inputs):
        scene_feat, scene_send, scene_source, scene_cot = inputs
        brick_count = scene_feat.shape[0]
        chan_one = scene_feat.shape[-1]
        chan_two = scene_cot.shape[-1]
        grid_one = scene_feat.reshape(brick_count, 8, 8, 8, chan_one)
        taps_one = shift_taps(grid_one, scene_rims(grid_one, scene_send, scene_source))
        pre_one = conv_apply(taps_one, conv_one)
        hidden_one = (scene_feat.reshape(-1, chan_one).astype(jnp.float32) + jax.nn.silu(pre_one)).astype(jnp.bfloat16)
        patches = down_rows(hidden_one, brick_count, chan_one)
        coarse = jnp.dot(patches, down_weight, preferred_element_type=jnp.float32).astype(jnp.bfloat16)
        grid_two = coarse.reshape(brick_count, 4, 4, 4, chan_two)
        taps_two = shift_taps(grid_two, scene_rims(grid_two, scene_send, scene_source))
        pre_two = conv_apply(taps_two, conv_two)
        encoded = (coarse.astype(jnp.float32) + jax.nn.silu(pre_two)).astype(jnp.bfloat16)
        upstream = scene_cot.reshape(-1, chan_two).astype(jnp.float32)
        delta_two = (upstream * silu_slope(pre_two)).astype(jnp.bfloat16)
        grid_delta = delta_two.reshape(brick_count, 4, 4, 4, chan_two)
        taps_delta = shift_taps(grid_delta, scene_rims(grid_delta, scene_send, scene_source))
        grad_coarse = (upstream + conv_back(taps_delta, conv_two)).astype(jnp.bfloat16)
        patch_grad = lax.dot_general(grad_coarse, down_weight, (((1,), (1,)), ((), ())), preferred_element_type=jnp.float32)
        delta_one = (up_rows(patch_grad, brick_count, chan_one) * silu_slope(pre_one)).astype(jnp.bfloat16)
        grad_one, grad_down, grad_two = carry
        grad_one = grad_one + weight_grads(taps_one, delta_one)
        grad_down = grad_down + lax.dot_general(patches, grad_coarse, (((0,), (0,)), ((), ())), preferred_element_type=jnp.float32)
        grad_two = grad_two + weight_grads(taps_two, delta_two)
        return (grad_one, grad_down, grad_two), encoded.reshape(brick_count, 64, chan_two)

    start = (jnp.zeros((7, C1, C1), jnp.float32), jnp.zeros((8 * C1, C2), jnp.float32), jnp.zeros((7, C2, C2), jnp.float32))
    grads, encoded = lax.scan(scene_pass, start, (features, send_faces, face_source, cotangent))
    return encoded, grads[0], grads[1], grads[2]
```

```python
import jax
import jax.numpy as jnp
from jax import lax
from jax.sharding import PartitionSpec as P

OPPOSITE = (0, 2, 1, 4, 3, 6, 5)


def swapped(value, axis, stride):
    mask = 2**stride
    pairs = [(source, source ^ mask) for source in range(lax.axis_size(axis))]
    return lax.ppermute(value, axis, pairs)


def face_slabs(blocks):
    return jnp.stack(
        [
            blocks[:, 0],
            blocks[:, -1],
            blocks[:, :, 0],
            blocks[:, :, -1],
            blocks[:, :, :, 0],
            blocks[:, :, :, -1],
        ],
        axis=1,
    )


def shift_taps(blocks, border):
    return [
        blocks,
        jnp.concatenate([border[:, 0][:, None], blocks[:, :-1]], 1),
        jnp.concatenate([blocks[:, 1:], border[:, 1][:, None]], 1),
        jnp.concatenate([border[:, 2][:, :, None], blocks[:, :, :-1]], 2),
        jnp.concatenate([blocks[:, :, 1:], border[:, 3][:, :, None]], 2),
        jnp.concatenate([border[:, 4][:, :, :, None], blocks[:, :, :, :-1]], 3),
        jnp.concatenate([blocks[:, :, :, 1:], border[:, 5][:, :, :, None]], 3),
    ]


def conv_apply(taps, weight):
    chans = taps[0].shape[-1]
    total = jnp.dot(taps[0].reshape(-1, chans), weight[0], preferred_element_type=jnp.float32)
    for tap_index in range(1, 7):
        total = total + jnp.dot(
            taps[tap_index].reshape(-1, chans),
            weight[tap_index],
            preferred_element_type=jnp.float32,
        )
    return total


def conv_back(taps, weight):
    chans = taps[0].shape[-1]
    total = lax.dot_general(
        taps[0].reshape(-1, chans),
        weight[0],
        (((1,), (1,)), ((), ())),
        preferred_element_type=jnp.float32,
    )
    for tap_index in range(1, 7):
        total = total + lax.dot_general(
            taps[OPPOSITE[tap_index]].reshape(-1, chans),
            weight[tap_index],
            (((1,), (1,)), ((), ())),
            preferred_element_type=jnp.float32,
        )
    return total


def weight_grads(taps, delta):
    chans = taps[0].shape[-1]
    return jnp.stack(
        [
            lax.dot_general(
                single.reshape(-1, chans),
                delta,
                (((0,), (0,)), ((), ())),
                preferred_element_type=jnp.float32,
            )
            for single in taps
        ]
    )


def down_rows(hidden, brick_count, chans):
    return (
        hidden.reshape(brick_count, 4, 2, 4, 2, 4, 2, chans)
        .transpose(0, 1, 3, 5, 2, 4, 6, 7)
        .reshape(brick_count * 64, 8 * chans)
    )


def up_rows(patch_grad, brick_count, chans):
    return (
        patch_grad.reshape(brick_count, 4, 4, 4, 2, 2, 2, chans)
        .transpose(0, 1, 4, 2, 5, 3, 6, 7)
        .reshape(brick_count * 512, chans)
    )


def silu_slope(value):
    sigma = jax.nn.sigmoid(value)
    return sigma * (1.0 + value * (1.0 - sigma))


def rims_local(blocks, send_list, source_list, swapper):
    brick_count = blocks.shape[0]
    side_cells = blocks.shape[1]
    chans = blocks.shape[-1]
    faces = face_slabs(blocks).reshape(brick_count * 6, side_cells, side_cells, chans)
    pieces = [faces]
    for bit_index in range(send_list.shape[0]):
        pieces.append(swapper(faces[send_list[bit_index]], bit_index))
    pieces.append(jnp.zeros((1, side_cells, side_cells, chans), faces.dtype))
    lookup = jnp.concatenate(pieces, axis=0)
    return lookup[source_list.reshape(-1)].reshape(brick_count, 6, side_cells, side_cells, chans)


CHUNK = 208
PLANE = 16


def plane_groups():
    return [[2 * chip + core for chip in range(PLANE)] for core in range(2)]


def summed(grad_one, grad_down, grad_two):
    core = lax.rem(lax.axis_index("scene"), 2)
    halves = [
        jnp.concatenate(
            [
                grad_one.reshape(2, 448, 128)[half],
                grad_down[:, 128 * half : 128 * half + 128],
                grad_two.reshape(1792, 256)[:, 128 * half : 128 * half + 128],
                jnp.zeros((64, 128), jnp.float32),
            ]
        )
        for half in range(2)
    ]
    kept = jnp.where(core == 0, halves[0], halves[1])
    sent = jnp.where(core == 0, halves[1], halves[0])
    mine = kept + swapped(sent, "scene", 0)
    groups = plane_groups()
    parts = mine.astype(jnp.bfloat16).reshape(PLANE, CHUNK, 128)
    parts = lax.all_to_all(parts, "scene", 0, 0, axis_index_groups=groups)
    piece = parts.astype(jnp.float32).sum(0).astype(jnp.bfloat16)
    pieces = lax.all_to_all(jnp.broadcast_to(piece[None], (8, CHUNK, 128)), "kd", 0, 0)
    piece = pieces.astype(jnp.float32).sum(0).astype(jnp.bfloat16)
    whole = lax.all_to_all(
        jnp.broadcast_to(piece[None], (PLANE, CHUNK, 128)), "scene", 0, 0, axis_index_groups=groups
    ).reshape(PLANE * CHUNK, 128)
    other = swapped(whole, "scene", 0)
    first = jnp.where(core == 0, whole, other).astype(jnp.float32)
    second = jnp.where(core == 0, other, whole).astype(jnp.float32)
    one = jnp.concatenate([first[:448], second[:448]]).reshape(7, 128, 128)
    down = jnp.concatenate([first[448:1472], second[448:1472]], axis=1)
    two = jnp.concatenate([first[1472:3264], second[1472:3264]], axis=1).reshape(7, 256, 256)
    return one, down, two


def on_device(features, send_faces, face_source, cotangent, conv_one, down_weight, conv_two):
    send_list = send_faces[0, 0]
    source_list = face_source[0]
    brick_count = features.shape[1]
    chan_one = features.shape[3]
    chan_two = cotangent.shape[3]
    grid_one = features[0].reshape(brick_count, 8, 8, 8, chan_one)
    border_one = rims_local(
        grid_one, send_list, source_list, lambda buffer, bit_index: swapped(buffer, "kd", bit_index)
    )
    taps_one = shift_taps(grid_one, border_one)
    pre_one = conv_apply(taps_one, conv_one)
    hidden_one = (
        features[0].reshape(-1, chan_one).astype(jnp.float32) + jax.nn.silu(pre_one)
    ).astype(jnp.bfloat16)
    patches = down_rows(hidden_one, brick_count, chan_one)
    coarse = jnp.dot(patches, down_weight, preferred_element_type=jnp.float32).astype(jnp.bfloat16)
    grid_two = coarse.reshape(brick_count, 4, 4, 4, chan_two)
    border_two = rims_local(
        grid_two, send_list, source_list, lambda buffer, bit_index: swapped(buffer, "kd", bit_index)
    )
    taps_two = shift_taps(grid_two, border_two)
    pre_two = conv_apply(taps_two, conv_two)
    encoded = (coarse.astype(jnp.float32) + jax.nn.silu(pre_two)).astype(jnp.bfloat16)
    upstream = cotangent[0].reshape(-1, chan_two).astype(jnp.float32)
    delta_two = (upstream * silu_slope(pre_two)).astype(jnp.bfloat16)
    grid_delta = delta_two.reshape(brick_count, 4, 4, 4, chan_two)
    border_delta = rims_local(
        grid_delta,
        send_list,
        source_list,
        lambda buffer, bit_index: swapped(buffer, "kd", bit_index),
    )
    taps_delta = shift_taps(grid_delta, border_delta)
    grad_two = weight_grads(taps_two, delta_two)
    grad_coarse = (upstream + conv_back(taps_delta, conv_two)).astype(jnp.bfloat16)
    grad_down = lax.dot_general(
        patches, grad_coarse, (((0,), (0,)), ((), ())), preferred_element_type=jnp.float32
    )
    patch_grad = lax.dot_general(
        grad_coarse, down_weight, (((1,), (1,)), ((), ())), preferred_element_type=jnp.float32
    )
    delta_one = (up_rows(patch_grad, brick_count, chan_one) * silu_slope(pre_one)).astype(
        jnp.bfloat16
    )
    grad_one = weight_grads(taps_one, delta_one)
    grad_one, grad_down, grad_two = summed(grad_one, grad_down, grad_two)
    return (encoded.reshape(1, brick_count, 64, chan_two), grad_one, grad_down, grad_two)


def solution(mesh):
    placed = (
        P("scene", "kd", None, None),
        P("scene", "kd", None, None),
        P("scene", "kd", None),
        P("scene", "kd", None, None),
        P(),
        P(),
        P(),
    )
    return jax.shard_map(
        on_device,
        mesh=mesh,
        in_specs=placed,
        out_specs=(P("scene", "kd", None, None), P(), P(), P()),
        check_vma=False,
    )
```

```python
import functools

import jax
import jax.numpy as jnp
from jax import lax
from jax.experimental import pallas as pl
from jax.experimental.pallas import tpu as pltpu
from jax.sharding import PartitionSpec as P

OPPOSITE = (0, 2, 1, 4, 3, 6, 5)
BRICKS = 4
C1 = 128
C2 = 256
LOCAL = 6 * BRICKS
EMPTY = LOCAL + 3
PLANE = 16
DEPTH = 8
CHUNK = 208
ONE_ROWS = 448
DOWN_ROWS = 1024
TWO_ROWS = 1792
EARLY = ONE_ROWS + DOWN_ROWS
HALF = EARLY + TWO_ROWS
F32 = jnp.float32
BF16 = jnp.bfloat16


def vmem():
    return pl.BlockSpec(memory_space=pltpu.VMEM)


def smem():
    return pl.BlockSpec(memory_space=pltpu.SMEM)


def call(body, scalars, arrays, outs, scratch=(), name=None):
    return pl.pallas_call(
        body,
        out_shape=[jax.ShapeDtypeStruct(shape, dtype) for shape, dtype in outs],
        in_specs=[smem() for _ in scalars] + [vmem() for _ in arrays],
        out_specs=[vmem() for _ in outs],
        scratch_shapes=list(scratch),
        compiler_params=pltpu.CompilerParams(vmem_limit_bytes=LIMIT),
        name=name,
    )(*scalars, *arrays)


LIMIT = 24 * 1024 * 1024


def nt_dot(left, right):
    return lax.dot_general(left, right, (((1,), (1,)), ((), ())), preferred_element_type=F32)


def tn_dot(left, right):
    return lax.dot_general(left, right, (((0,), (0,)), ((), ())), preferred_element_type=F32)


def face_value(ref, base, edge, axis, upper):
    area = edge * edge
    if axis == 0:
        return ref[pl.ds(base + upper * (edge * area - area), area), :]
    if axis == 1:
        return jnp.concatenate(
            [ref[pl.ds(base + row * area + upper * (area - edge), edge), :] for row in range(edge)]
        )
    return ref[pl.ds(base + upper * (edge - 1), area, stride=edge), :]


def write_face(ref, base, edge, axis, upper, value):
    area = edge * edge
    if axis == 0:
        ref[pl.ds(base + upper * (edge * area - area), area), :] = value
    elif axis == 1:
        for row in range(edge):
            ref[pl.ds(base + row * area + upper * (area - edge), edge), :] = value[
                row * edge : row * edge + edge
            ]
    else:
        ref[pl.ds(base + upper * (edge - 1), area, stride=edge), :] = value


def sent_face(ref, send_ref, edge, axis):
    face = send_ref[0, 0, axis, 0]
    brick = lax.div(face, 6)
    upper = lax.rem(face, 2)
    return face_value(ref, pl.multiple_of(brick * edge**3, edge**3), edge, axis, upper)


def write_tap(out, field, source_ref, received, edge, side):
    volume = edge**3
    total = BRICKS * volume
    axis, upper = side // 2, side % 2
    step = edge ** (2 - axis)
    if upper:
        out[pl.ds(0, total - step), :] = field[pl.ds(step, total - step), :]
    else:
        out[pl.ds(step, total - step), :] = field[pl.ds(0, total - step), :]
    border = received[axis][...].astype(F32)
    for brick in range(BRICKS):
        source = source_ref[0, brick, side]
        near = lax.div(jnp.minimum(source, LOCAL - 1), 6)
        slab = face_value(field, pl.multiple_of(near * volume, volume), edge, axis, 1 - upper)
        rim = jnp.where(
            source < LOCAL, slab, jnp.where(source < EMPTY, border, jnp.zeros_like(border))
        )
        write_face(out, brick * volume, edge, axis, upper, rim)


def sigmoid(value):
    return 1.0 / (1.0 + jnp.exp(-value))


def feature_faces(send_ref, features, face_0, face_1, face_2, brick_ref):
    for axis, out in enumerate((face_0, face_1, face_2)):
        face = send_ref[0, 0, axis, 0]
        base = pl.multiple_of(lax.div(face, 6) * 512, 512)
        upper = lax.rem(face, 2)
        brick_ref[axis] = features[pl.ds(base, 512), :].astype(F32)
        out[...] = face_value(brick_ref.at[axis], 0, 8, axis, upper).astype(BF16)


def level_one(
    source_ref, send_ref, features, got_0, got_1, got_2, weight, down,
    taps, slope, patches, coarse, face_0, face_1, face_2,
    field, shifted, hidden, cells,
):
    field[...] = features[...].astype(F32)
    taps[:, 0:C1] = features[...]
    for side in range(6):
        tap = shifted.at[side]
        write_tap(tap, field, source_ref, (got_0, got_1, got_2), 8, side)
        taps[:, C1 * (side + 1) : C1 * (side + 2)] = tap[...].astype(BF16)
    for brick in range(BRICKS):
        rows = pl.ds(512 * brick, 512)
        pre = jnp.dot(taps[rows, :], weight[...], preferred_element_type=F32)
        gate = sigmoid(pre)
        slope[rows, :] = gate * (1.0 + pre * (1.0 - gate))
        hidden[rows, :] = field[rows, :] + pre * gate
    low = lax.broadcasted_iota(jnp.int32, (1, 8, C1), 1) < 4
    for r in range(2):
        rows = hidden[pl.ds(r, 1024, stride=2), :].reshape(BRICKS * 4, 2, 2, 2, 8, C1)
        for a in range(2):
            left = rows[:, a, :, 0].reshape(32, 8, C1)
            right = rows[:, a, :, 1].reshape(32, 8, C1)
            first = jnp.where(low, left, pltpu.roll(right, 4, 1))
            second = jnp.where(low, pltpu.roll(left, 4, 1), right)
            for q, value in enumerate((first, second)):
                lane = ((a * 2 + q) * 2 + r) * C1
                patches[:, lane : lane + C1] = value.reshape(256, C1).astype(BF16)
    low_res = jnp.dot(patches[...], down[...], preferred_element_type=F32).astype(BF16)
    coarse[...] = low_res
    cells[0] = low_res[:, :C1].astype(F32)
    cells[1] = low_res[:, C1:].astype(F32)
    for axis, out in enumerate((face_0, face_1, face_2)):
        for part in range(2):
            out[:, C1 * part : C1 * part + C1] = sent_face(
                cells.at[part], send_ref, 4, axis
            ).astype(BF16)


def level_two_taps(source_ref, received, cells, shifted, taps):
    for side in range(6):
        for part in range(2):
            tap = shifted.at[side, part]
            lanes = pl.ds(C1 * part, C1)
            write_tap(
                tap, cells.at[part], source_ref, tuple(got.at[:, lanes] for got in received), 4, side
            )
            start = C2 * (side + 1) + C1 * part
            taps[:, start : start + C1] = tap[...].astype(BF16)


def level_two(
    source_ref, send_ref, coarse, got_0, got_1, got_2, weight, cotangent,
    taps, encoded, delta, face_0, face_1, face_2,
    cells, shifted,
):
    low_res = coarse[...]
    cells[0] = low_res[:, :C1].astype(F32)
    cells[1] = low_res[:, C1:].astype(F32)
    taps[:, 0:C2] = low_res
    level_two_taps(source_ref, (got_0, got_1, got_2), cells, shifted, taps)
    pre = jnp.dot(taps[...], weight[...], preferred_element_type=F32)
    gate = sigmoid(pre)
    encoded[...] = (low_res.astype(F32) + pre * gate).astype(BF16)
    change = (cotangent[...].astype(F32) * (gate * (1.0 + pre * (1.0 - gate)))).astype(BF16)
    delta[...] = change
    cells[0] = change[:, :C1].astype(F32)
    cells[1] = change[:, C1:].astype(F32)
    for axis, out in enumerate((face_0, face_1, face_2)):
        for part in range(2):
            out[:, C1 * part : C1 * part + C1] = sent_face(
                cells.at[part], send_ref, 4, axis
            ).astype(BF16)


def core_index():
    return lax.rem(lax.axis_index("scene"), 2)


def two_gradient(taps, delta, kept, sent, both):
    change = delta[...]
    for tap in range(7):
        grad = tn_dot(taps[:, C2 * tap : C2 * tap + C2], change)
        rows = pl.ds(C2 * tap, C2)
        both[0, rows, :] = grad[:, :C1]
        both[1, rows, :] = grad[:, C1:]
    core = core_index()
    kept[...] = both[core]
    sent[...] = both[1 - core].astype(BF16)


def backward(
    source_ref, delta, got_0, got_1, got_2, weight, cotangent, down, patches, slope, taps_one,
    kept, sent,
    cells, shifted, taps, patch_grad, spread, delta_one, both,
):
    change = delta[...]
    cells[0] = change[:, :C1].astype(F32)
    cells[1] = change[:, C1:].astype(F32)
    taps[:, 0:C2] = change
    level_two_taps(source_ref, (got_0, got_1, got_2), cells, shifted, taps)
    total = cotangent[...].astype(F32)
    for tap in range(7):
        lane = C2 * OPPOSITE[tap]
        total = total + nt_dot(taps[:, lane : lane + C2], weight[pl.ds(C2 * tap, C2), :])
    upstream = total.astype(BF16)
    grad_down = tn_dot(patches[...], upstream)
    both[0, pl.ds(ONE_ROWS, DOWN_ROWS), :] = grad_down[:, :C1]
    both[1, pl.ds(ONE_ROWS, DOWN_ROWS), :] = grad_down[:, C1:]
    patch_grad[...] = nt_dot(upstream, down[...])
    low = lax.broadcasted_iota(jnp.int32, (1, 8, C1), 1) < 4
    for r in range(2):
        halves = []
        for a in range(2):
            lane = (a * 4 + r) * C1
            first = patch_grad[:, lane : lane + C1].reshape(32, 8, C1)
            lane = lane + 2 * C1
            second = patch_grad[:, lane : lane + C1].reshape(32, 8, C1)
            left = jnp.where(low, first, pltpu.roll(second, 4, 1))
            right = jnp.where(low, pltpu.roll(first, 4, 1), second)
            halves.append(jnp.stack([left, right], axis=1).reshape(BRICKS * 4, 4, 8, C1))
        spread[pl.ds(r, 1024, stride=2), :] = jnp.stack(halves, axis=1).reshape(1024, C1)
    delta_one[...] = (spread[...] * slope[...]).astype(BF16)
    grad_one = tn_dot(delta_one[...], taps_one[...])
    for tap in range(7):
        block = grad_one[:, C1 * tap : C1 * tap + C1].T
        for start in range(0, C1, 64):
            row = C1 * tap + start
            both[row // ONE_ROWS, pl.ds(row % ONE_ROWS, 64), :] = block[start : start + 64]
    core = core_index()
    kept[...] = both[core]
    sent[...] = both[1 - core].astype(BF16)


def pair_sum(kept_a, got_a, kept_b, got_b, out):
    out[pl.ds(0, EARLY), :] = (kept_a[...] + got_a[...].astype(F32)).astype(BF16)
    out[pl.ds(EARLY, TWO_ROWS), :] = (kept_b[...] + got_b[...].astype(F32)).astype(BF16)
    out[pl.ds(HALF, PLANE * CHUNK - HALF), :] = jnp.zeros((PLANE * CHUNK - HALF, C1), BF16)


def group_sum(parts, out):
    total = parts[0].astype(F32)
    for index in range(1, parts.shape[0]):
        total = total + parts[index].astype(F32)
    total = total.astype(BF16)
    for index in range(out.shape[0]):
        out[index] = total


def unpack(own, other, one, down, two):
    def write(first, second):
        one[pl.ds(0, ONE_ROWS), :] = first[pl.ds(0, ONE_ROWS), :].astype(F32)
        one[pl.ds(ONE_ROWS, ONE_ROWS), :] = second[pl.ds(0, ONE_ROWS), :].astype(F32)
        for half, source in enumerate((first, second)):
            lanes = slice(C1 * half, C1 * half + C1)
            down[:, lanes] = source[pl.ds(ONE_ROWS, DOWN_ROWS), :].astype(F32)
            two[:, lanes] = source[pl.ds(EARLY, TWO_ROWS), :].astype(F32)

    core = core_index()

    @pl.when(core == 0)
    def _():
        write(own, other)

    @pl.when(core == 1)
    def _():
        write(other, own)


def swapped(value, axis, bit):
    mask = 2**bit
    pairs = [(source, source ^ mask) for source in range(lax.axis_size(axis))]
    return lax.ppermute(value, axis, pairs)


def exchanged(faces):
    return [swapped(face, "kd", bit) for bit, face in enumerate(faces)]


def on_device(features, send_faces, face_source, cotangent, conv_one, down_weight, conv_two):
    field = features.reshape(2048, C1)
    upstream = cotangent.reshape(256, C2)
    weight_one = conv_one.reshape(7 * C1, C1)
    weight_two = conv_two.reshape(7 * C2, C2)
    sent = call(
        feature_faces, (send_faces,), (field,), [((64, C1), BF16)] * 3,
        [pltpu.VMEM((3, 512, C1), F32)], "feature_faces",
    )
    taps_one, slope, patches, coarse, *sent = call(
        level_one, (face_source, send_faces), (field, *exchanged(sent), weight_one, down_weight),
        [((2048, 7 * C1), BF16), ((2048, C1), F32), ((256, 8 * C1), BF16), ((256, C2), BF16)]
        + [((16, C2), BF16)] * 3,
        [
            pltpu.VMEM((2048, C1), F32),
            pltpu.VMEM((6, 2048, C1), F32),
            pltpu.VMEM((2048, C1), F32),
            pltpu.VMEM((2, 256, C1), F32),
        ],
        "level_one",
    )
    taps_two, encoded, delta, *sent = call(
        level_two, (face_source, send_faces), (coarse, *exchanged(sent), weight_two, upstream),
        [((256, 7 * C2), BF16), ((256, C2), BF16), ((256, C2), BF16)] + [((16, C2), BF16)] * 3,
        [pltpu.VMEM((2, 256, C1), F32), pltpu.VMEM((6, 2, 256, C1), F32)],
        "level_two",
    )
    received = exchanged(sent)
    kept_two, sent_two = call(
        two_gradient, (), (taps_two, delta), [((TWO_ROWS, C1), F32), ((TWO_ROWS, C1), BF16)],
        [pltpu.VMEM((2, TWO_ROWS, C1), F32)], "two_gradient",
    )
    got_two = swapped(sent_two, "scene", 0)
    kept, sent = call(
        backward, (face_source,),
        (delta, *received, weight_two, upstream, down_weight, patches, slope, taps_one),
        [((EARLY, C1), F32), ((EARLY, C1), BF16)],
        [
            pltpu.VMEM((2, 256, C1), F32),
            pltpu.VMEM((6, 2, 256, C1), F32),
            pltpu.VMEM((256, 7 * C2), BF16),
            pltpu.VMEM((256, 8 * C1), F32),
            pltpu.VMEM((2048, C1), F32),
            pltpu.VMEM((2048, C1), BF16),
            pltpu.VMEM((2, EARLY, C1), F32),
        ],
        "backward",
    )
    got = swapped(sent, "scene", 0)
    groups = [[2 * chip + core for chip in range(PLANE)] for core in range(2)]
    (packed,) = call(
        pair_sum, (), (kept, got, kept_two, got_two), [((PLANE * CHUNK, C1), BF16)], (), "pair_sum"
    )
    parts = lax.all_to_all(
        packed.reshape(PLANE, CHUNK, C1), "scene", 0, 0, axis_index_groups=groups
    )
    (copies,) = call(group_sum, (), (parts,), [((DEPTH, CHUNK, C1), BF16)], (), "plane_sum")
    parts = lax.all_to_all(copies, "kd", 0, 0)
    (copies,) = call(group_sum, (), (parts,), [((PLANE, CHUNK, C1), BF16)], (), "depth_sum")
    own = lax.all_to_all(copies, "scene", 0, 0, axis_index_groups=groups)
    own = own.reshape(PLANE * CHUNK, C1)
    other = swapped(own, "scene", 0)
    one, down, two = call(
        unpack, (), (own, other),
        [((7 * C1, C1), F32), ((8 * C1, C2), F32), ((7 * C2, C2), F32)], (), "unpack",
    )
    return (
        encoded.reshape(1, BRICKS, 64, C2),
        one.reshape(7, C1, C1),
        down,
        two.reshape(7, C2, C2),
    )


def solution(mesh):
    placed = (
        P("scene", "kd", None, None),
        P("scene", "kd", None, None),
        P("scene", "kd", None),
        P("scene", "kd", None, None),
        P(),
        P(),
        P(),
    )
    return jax.shard_map(
        on_device,
        mesh=mesh,
        in_specs=placed,
        out_specs=(P("scene", "kd", None, None), P(), P(), P()),
        check_vma=False,
    )
```

```python
import functools

import jax
import jax.numpy as jnp
from jax import lax
from jax.experimental import pallas as pl
from jax.experimental.pallas import tpu as pltpu
from jax.sharding import PartitionSpec as P


OPPOSITE = (0, 2, 1, 4, 3, 6, 5)
BRICKS = 4
C1 = 128
C2 = 256
LOCAL = 6 * BRICKS
EMPTY = LOCAL + 3
PLANE = 16
DEPTH = 8
CHUNK = 208
ONE_ROWS = 448
DOWN_ROWS = 1024
TWO_ROWS = 1792
EARLY = ONE_ROWS + DOWN_ROWS
HALF = EARLY + TWO_ROWS
F32 = jnp.float32
BF16 = jnp.bfloat16


def vmem():
    return pl.BlockSpec(memory_space=pltpu.VMEM)


def smem():
    return pl.BlockSpec(memory_space=pltpu.SMEM)


def hbm():
    return pl.BlockSpec(memory_space=pltpu.HBM)


LIMIT = 24 * 1024 * 1024


def call(body, inputs, outs, scratch=(), aliases=None):
    return pl.pallas_call(
        body,
        out_shape=[jax.ShapeDtypeStruct(shape, dtype) for _, shape, dtype in outs],
        in_specs=[place() for place, _ in inputs],
        out_specs=[place() for place, _, _ in outs],
        scratch_shapes=list(scratch),
        input_output_aliases=aliases or {},
        compiler_params=pltpu.CompilerParams(vmem_limit_bytes=LIMIT),
    )(*[value for _, value in inputs])


def begin(sem, *pairs):
    copies = [
        pltpu.make_async_copy(source, target, sem.at[index])
        for index, (source, target) in enumerate(pairs)
    ]
    for copy in copies:
        copy.start()
    return copies


def nt_dot(left, right):
    return lax.dot_general(left, right, (((1,), (1,)), ((), ())), preferred_element_type=F32)


def tn_dot(left, right):
    return lax.dot_general(left, right, (((0,), (0,)), ((), ())), preferred_element_type=F32)


def face_value(ref, base, edge, axis, upper):
    area = edge * edge
    if axis == 0:
        return ref[pl.ds(base + upper * (edge * area - area), area), :]
    if axis == 1:
        return jnp.concatenate(
            [ref[pl.ds(base + row * area + upper * (area - edge), edge), :] for row in range(edge)]
        )
    return ref[pl.ds(base + upper * (edge - 1), area, stride=edge), :]


def write_face(ref, base, edge, axis, upper, value):
    area = edge * edge
    if axis == 0:
        ref[pl.ds(base + upper * (edge * area - area), area), :] = value
    elif axis == 1:
        for row in range(edge):
            ref[pl.ds(base + row * area + upper * (area - edge), edge), :] = value[
                row * edge : row * edge + edge
            ]
    else:
        ref[pl.ds(base + upper * (edge - 1), area, stride=edge), :] = value


def sent_face(ref, send_ref, edge, axis):
    face = send_ref[0, axis]
    brick = lax.div(face, 6)
    upper = lax.rem(face, 2)
    return face_value(ref, pl.multiple_of(brick * edge**3, edge**3), edge, axis, upper)


def write_tap(out, field, source_ref, received, edge, side):
    volume = edge**3
    total = BRICKS * volume
    axis, upper = side // 2, side % 2
    step = edge ** (2 - axis)
    if upper:
        out[pl.ds(0, total - step), :] = field[pl.ds(step, total - step), :]
    else:
        out[pl.ds(step, total - step), :] = field[pl.ds(0, total - step), :]
    border = received[axis][...].astype(F32)
    for brick in range(BRICKS):
        source = source_ref[0, brick, side]
        near = lax.div(jnp.minimum(source, LOCAL - 1), 6)
        slab = face_value(field, pl.multiple_of(near * volume, volume), edge, axis, 1 - upper)
        rim = jnp.where(
            source < LOCAL, slab, jnp.where(source < EMPTY, border, jnp.zeros_like(border))
        )
        write_face(out, brick * volume, edge, axis, upper, rim)


def sigmoid(value):
    return 1.0 / (1.0 + jnp.exp(-value))


def feature_faces(
    features, sides, sources, field, source_out, face_0, face_1, face_2, send_ref, brick_ref, sem
):
    copies = begin(sem, (sides, send_ref), (features, field), (sources, source_out))
    for copy in copies:
        copy.wait()
    for axis, out in enumerate((face_0, face_1, face_2)):
        face = send_ref[0, axis]
        base = pl.multiple_of(lax.div(face, 6) * 512, 512)
        brick_ref[axis] = field[pl.ds(base, 512), :].astype(F32)
        out[...] = face_value(brick_ref.at[axis], 0, 8, axis, lax.rem(face, 2)).astype(BF16)


def level_one(
    source_ref, send_ref, features, got_0, got_1, got_2, conv, down_far, conv_next, cot_far,
    taps, slope, patches, coarse, face_0, face_1, face_2, down, weight_next, cotangent,
    field, shifted, hidden, cells, weight, sem,
):
    copies = begin(
        sem, (conv, weight), (down_far, down), (conv_next, weight_next), (cot_far, cotangent)
    )
    field[...] = features[...].astype(F32)
    taps[:, 0:C1] = features[...]
    for side in range(6):
        tap = shifted.at[side]
        write_tap(tap, field, source_ref, (got_0, got_1, got_2), 8, side)
        taps[:, C1 * (side + 1) : C1 * (side + 2)] = tap[...].astype(BF16)
    copies[0].wait()
    for brick in range(BRICKS):
        rows = pl.ds(512 * brick, 512)
        pre = jnp.dot(taps[rows, :], weight[...], preferred_element_type=F32)
        gate = sigmoid(pre)
        slope[rows, :] = gate * (1.0 + pre * (1.0 - gate))
        hidden[rows, :] = field[rows, :] + pre * gate
    low = lax.broadcasted_iota(jnp.int32, (1, 8, C1), 1) < 4
    for r in range(2):
        rows = hidden[pl.ds(r, 1024, stride=2), :].reshape(BRICKS * 4, 2, 2, 2, 8, C1)
        for a in range(2):
            left = rows[:, a, :, 0].reshape(32, 8, C1)
            right = rows[:, a, :, 1].reshape(32, 8, C1)
            first = jnp.where(low, left, pltpu.roll(right, 4, 1))
            second = jnp.where(low, pltpu.roll(left, 4, 1), right)
            for q, value in enumerate((first, second)):
                lane = ((a * 2 + q) * 2 + r) * C1
                patches[:, lane : lane + C1] = value.reshape(256, C1).astype(BF16)
    copies[1].wait()
    low_res = jnp.dot(patches[...], down[...], preferred_element_type=F32).astype(BF16)
    coarse[...] = low_res
    cells[0] = low_res[:, :C1].astype(F32)
    cells[1] = low_res[:, C1:].astype(F32)
    for axis, out in enumerate((face_0, face_1, face_2)):
        for part in range(2):
            out[:, C1 * part : C1 * part + C1] = sent_face(
                cells.at[part], send_ref, 4, axis
            ).astype(BF16)
    for copy in copies[2:]:
        copy.wait()


def level_two_taps(source_ref, received, cells, shifted, taps):
    for side in range(6):
        for part in range(2):
            tap = shifted.at[side, part]
            lanes = pl.ds(C1 * part, C1)
            write_tap(
                tap, cells.at[part], source_ref, tuple(got.at[:, lanes] for got in received), 4, side
            )
            start = C2 * (side + 1) + C1 * part
            taps[:, start : start + C1] = tap[...].astype(BF16)


def level_two(
    source_ref, send_ref, coarse, got_0, got_1, got_2, weight, cotangent,
    taps, bent, delta, face_0, face_1, face_2,
    cells, shifted,
):
    low_res = coarse[...]
    cells[0] = low_res[:, :C1].astype(F32)
    cells[1] = low_res[:, C1:].astype(F32)
    taps[:, 0:C2] = low_res
    level_two_taps(source_ref, (got_0, got_1, got_2), cells, shifted, taps)
    pre = jnp.dot(taps[...], weight[...], preferred_element_type=F32)
    gate = sigmoid(pre)
    bent[...] = pre * gate
    change = (cotangent[...].astype(F32) * (gate * (1.0 + pre * (1.0 - gate)))).astype(BF16)
    delta[...] = change
    cells[0] = change[:, :C1].astype(F32)
    cells[1] = change[:, C1:].astype(F32)
    for axis, out in enumerate((face_0, face_1, face_2)):
        for part in range(2):
            out[:, C1 * part : C1 * part + C1] = sent_face(
                cells.at[part], send_ref, 4, axis
            ).astype(BF16)


def core_index():
    return lax.rem(lax.axis_index("scene"), 2)


def two_gradient(taps, delta, coarse, bent, kept, sent, encoded, both):
    encoded[...] = (coarse[...].astype(F32) + bent[...]).astype(BF16)
    change = delta[...]
    for tap in range(7):
        grad = tn_dot(taps[:, C2 * tap : C2 * tap + C2], change)
        rows = pl.ds(C2 * tap, C2)
        both[0, rows, :] = grad[:, :C1]
        both[1, rows, :] = grad[:, C1:]
    core = core_index()
    kept[...] = both[core]
    sent[...] = both[1 - core].astype(BF16)


def backward(
    source_ref, delta, got_0, got_1, got_2, weight, cotangent, down, patches, slope, taps_one,
    kept, sent,
    cells, shifted, taps, patch_grad, spread, delta_one, both,
):
    change = delta[...]
    cells[0] = change[:, :C1].astype(F32)
    cells[1] = change[:, C1:].astype(F32)
    taps[:, 0:C2] = change
    level_two_taps(source_ref, (got_0, got_1, got_2), cells, shifted, taps)
    total = cotangent[...].astype(F32)
    for tap in range(7):
        lane = C2 * OPPOSITE[tap]
        total = total + nt_dot(taps[:, lane : lane + C2], weight[pl.ds(C2 * tap, C2), :])
    upstream = total.astype(BF16)
    grad_down = tn_dot(patches[...], upstream)
    both[0, pl.ds(ONE_ROWS, DOWN_ROWS), :] = grad_down[:, :C1]
    both[1, pl.ds(ONE_ROWS, DOWN_ROWS), :] = grad_down[:, C1:]
    patch_grad[...] = nt_dot(upstream, down[...])
    low = lax.broadcasted_iota(jnp.int32, (1, 8, C1), 1) < 4
    for r in range(2):
        halves = []
        for a in range(2):
            lane = (a * 4 + r) * C1
            first = patch_grad[:, lane : lane + C1].reshape(32, 8, C1)
            lane = lane + 2 * C1
            second = patch_grad[:, lane : lane + C1].reshape(32, 8, C1)
            left = jnp.where(low, first, pltpu.roll(second, 4, 1))
            right = jnp.where(low, pltpu.roll(first, 4, 1), second)
            halves.append(jnp.stack([left, right], axis=1).reshape(BRICKS * 4, 4, 8, C1))
        spread[pl.ds(r, 1024, stride=2), :] = jnp.stack(halves, axis=1).reshape(1024, C1)
    delta_one[...] = (spread[...] * slope[...]).astype(BF16)
    grad_one = tn_dot(delta_one[...], taps_one[...])
    for tap in range(7):
        block = grad_one[:, C1 * tap : C1 * tap + C1].T
        for start in range(0, C1, 64):
            row = C1 * tap + start
            both[row // ONE_ROWS, pl.ds(row % ONE_ROWS, 64), :] = block[start : start + 64]
    core = core_index()
    kept[...] = both[core]
    sent[...] = both[1 - core].astype(BF16)


def pair_sum(kept_a, got_a, kept_b, got_b, out):
    out[pl.ds(0, EARLY), :] = (kept_a[...] + got_a[...].astype(F32)).astype(BF16)
    out[pl.ds(EARLY, TWO_ROWS), :] = (kept_b[...] + got_b[...].astype(F32)).astype(BF16)
    out[pl.ds(HALF, PLANE * CHUNK - HALF), :] = jnp.zeros((PLANE * CHUNK - HALF, C1), BF16)


def group_sum(parts, out):
    total = parts[0].astype(F32)
    for index in range(1, parts.shape[0]):
        total = total + parts[index].astype(F32)
    total = total.astype(BF16)
    for index in range(out.shape[0]):
        out[index] = total


def unpack(turned, source, *refs):
    one, down, two, stage, sem = refs[-5:]
    half = core_index()
    if turned:
        half = 1 - half
    lanes = pl.ds(pl.multiple_of(half * C1, C1), C1)
    targets = (
        (EARLY, TWO_ROWS, two.at[:, lanes]),
        (ONE_ROWS, DOWN_ROWS, down.at[:, lanes]),
        (0, ONE_ROWS, one.at[pl.ds(pl.multiple_of(half * ONE_ROWS, ONE_ROWS), ONE_ROWS), :]),
    )
    copies = []
    for index, (start, size, target) in enumerate(targets):
        rows = pl.ds(start, size)
        stage[rows, :] = source[rows, :].astype(F32)
        copies.append(pltpu.make_async_copy(stage.at[rows, :], target, sem.at[index]))
        copies[-1].start()
    for copy in copies:
        copy.wait()


def swapped(value, axis, bit):
    mask = 2**bit
    pairs = [(source, source ^ mask) for source in range(lax.axis_size(axis))]
    return lax.ppermute(value, axis, pairs)


def exchanged(faces):
    got = []
    for bit, face in enumerate(faces):
        got.append(swapped(face, "kd", bit))
    return got


def step(features, send_faces, face_source, cotangent, conv_one, down_weight, conv_two):
    sides = send_faces.reshape(1, 3)
    weight_one = conv_one.reshape(7 * C1, C1)
    weight_two = conv_two.reshape(7 * C2, C2)
    dma = pltpu.SemaphoreType.DMA
    field, sources, *sent = call(
        feature_faces,
        [(hbm, features.reshape(2048, C1)), (hbm, sides), (hbm, face_source)],
        [(vmem, (2048, C1), BF16), (vmem, (1, BRICKS, 6), jnp.int32)]
        + [(vmem, (64, C1), BF16)] * 3,
        [pltpu.SMEM((1, 3), jnp.int32), pltpu.VMEM((3, 512, C1), F32), dma((3,))],
    )
    received = exchanged(sent)
    taps_one, slope, patches, coarse, face_0, face_1, face_2, down, weight, upstream = call(
        level_one,
        [(smem, sources), (smem, sides), (vmem, field)]
        + [(vmem, got) for got in received]
        + [(hbm, weight_one), (hbm, down_weight), (hbm, weight_two)]
        + [(hbm, cotangent.reshape(256, C2))],
        [
            (vmem, (2048, 7 * C1), BF16),
            (vmem, (2048, C1), F32),
            (vmem, (256, 8 * C1), BF16),
            (vmem, (256, C2), BF16),
        ]
        + [(vmem, (16, C2), BF16)] * 3
        + [(vmem, (8 * C1, C2), BF16), (vmem, (7 * C2, C2), BF16), (vmem, (256, C2), BF16)],
        [
            pltpu.VMEM((2048, C1), F32),
            pltpu.VMEM((6, 2048, C1), F32),
            pltpu.VMEM((2048, C1), F32),
            pltpu.VMEM((2, 256, C1), F32),
            pltpu.VMEM((7 * C1, C1), BF16),
            dma((4,)),
        ],
    )
    received = exchanged((face_0, face_1, face_2))
    taps_two, bent, delta, *sent = call(
        level_two,
        [(smem, sources), (smem, sides), (vmem, coarse)]
        + [(vmem, got) for got in received]
        + [(vmem, weight), (vmem, upstream)],
        [(vmem, (256, 7 * C2), BF16), (vmem, (256, C2), F32), (vmem, (256, C2), BF16)]
        + [(vmem, (16, C2), BF16)] * 3,
        [pltpu.VMEM((2, 256, C1), F32), pltpu.VMEM((6, 2, 256, C1), F32)],
    )
    received = exchanged(sent)
    kept_two, sent_two, encoded = call(
        two_gradient,
        [(vmem, taps_two), (vmem, delta), (vmem, coarse), (vmem, bent)],
        [(vmem, (TWO_ROWS, C1), F32), (vmem, (TWO_ROWS, C1), BF16), (vmem, (256, C2), BF16)],
        [pltpu.VMEM((2, TWO_ROWS, C1), F32)],
    )
    got_two = swapped(sent_two, "scene", 0)
    kept, sent = call(
        backward,
        [(smem, sources), (vmem, delta)]
        + [(vmem, got) for got in received]
        + [(vmem, weight), (vmem, upstream), (vmem, down), (vmem, patches), (vmem, slope)]
        + [(vmem, taps_one)],
        [(vmem, (EARLY, C1), F32), (vmem, (EARLY, C1), BF16)],
        [
            pltpu.VMEM((2, 256, C1), F32),
            pltpu.VMEM((6, 2, 256, C1), F32),
            pltpu.VMEM((256, 7 * C2), BF16),
            pltpu.VMEM((256, 8 * C1), F32),
            pltpu.VMEM((2048, C1), F32),
            pltpu.VMEM((2048, C1), BF16),
            pltpu.VMEM((2, EARLY, C1), F32),
        ],
    )
    got = swapped(sent, "scene", 0)
    groups = [[2 * chip + core for chip in range(PLANE)] for core in range(2)]
    (packed,) = call(
        pair_sum,
        [(vmem, kept), (vmem, got), (vmem, kept_two), (vmem, got_two)],
        [(vmem, (PLANE * CHUNK, C1), BF16)],
    )
    parts = lax.all_to_all(
        packed.reshape(PLANE, CHUNK, C1), "scene", 0, 0, axis_index_groups=groups
    )
    (copies,) = call(group_sum, [(vmem, parts)], [(vmem, (DEPTH, CHUNK, C1), BF16)])
    parts = lax.all_to_all(copies, "kd", 0, 0)
    (copies,) = call(group_sum, [(vmem, parts)], [(vmem, (PLANE, CHUNK, C1), BF16)])
    own = lax.all_to_all(copies, "scene", 0, 0, axis_index_groups=groups)
    own = own.reshape(PLANE * CHUNK, C1)
    other = swapped(own, "scene", 0)
    shapes = [(hbm, (7 * C1, C1), F32), (hbm, (8 * C1, C2), F32), (hbm, (7 * C2, C2), F32)]
    scratch = [pltpu.VMEM((HALF, C1), F32), dma((3,))]
    partial = call(functools.partial(unpack, False), [(vmem, own)], shapes, scratch)
    one, low, two = call(
        functools.partial(unpack, True),
        [(vmem, other)] + [(hbm, value) for value in partial],
        shapes,
        scratch,
        {1: 0, 2: 1, 3: 2},
    )
    return (
        encoded.reshape(1, BRICKS, 64, C2),
        one.reshape(7, C1, C1),
        low,
        two.reshape(7, C2, C2),
    )


def solution(mesh):
    placed = (
        P("scene", "kd", None, None),
        P("scene", "kd", None, None),
        P("scene", "kd", None),
        P("scene", "kd", None, None),
        P(),
        P(),
        P(),
    )
    return jax.shard_map(
        step,
        mesh=mesh,
        in_specs=placed,
        out_specs=(P("scene", "kd", None, None), P(), P(), P()),
        check_vma=False,
    )
```

```python
import functools

import jax
import jax.numpy as jnp
from jax import lax
from jax.experimental import pallas as pl
from jax.experimental.pallas import tpu as pltpu
from jax.sharding import PartitionSpec as P


OPPOSITE = (0, 2, 1, 4, 3, 6, 5)
BRICKS = 4
C1 = 128
C2 = 256
LOCAL = 6 * BRICKS
PLANE = 16
DEPTH = 8
CHUNK = 208
ONE_ROWS = 448
DOWN_ROWS = 1024
TWO_ROWS = 1792
EARLY = ONE_ROWS + DOWN_ROWS
HALF = EARLY + TWO_ROWS
F32 = jnp.float32
BF16 = jnp.bfloat16


def vmem():
    return pl.BlockSpec(memory_space=pltpu.VMEM)


def smem():
    return pl.BlockSpec(memory_space=pltpu.SMEM)


def hbm():
    return pl.BlockSpec(memory_space=pltpu.HBM)


LIMIT = 24 * 1024 * 1024


def far(value):
    return pltpu.with_memory_space_constraint(value, pltpu.HBM)


def call(body, inputs, outs, scratch=(), aliases=None):
    return pl.pallas_call(
        body,
        out_shape=[jax.ShapeDtypeStruct(shape, dtype) for _, shape, dtype in outs],
        in_specs=[place() for place, _ in inputs],
        out_specs=[place() for place, _, _ in outs],
        scratch_shapes=list(scratch),
        input_output_aliases=aliases or {},
        compiler_params=pltpu.CompilerParams(vmem_limit_bytes=LIMIT),
    )(*[far(value) if place is hbm else value for place, value in inputs])


def begin(sem, *pairs):
    copies = [
        pltpu.make_async_copy(source, target, sem.at[index])
        for index, (source, target) in enumerate(pairs)
    ]
    for copy in copies:
        copy.start()
    return copies


def nt_dot(left, right):
    return lax.dot_general(left, right, (((1,), (1,)), ((), ())), preferred_element_type=F32)


def tn_dot(left, right):
    return lax.dot_general(left, right, (((0,), (0,)), ((), ())), preferred_element_type=F32)


def face_value(ref, base, edge, axis, upper):
    area = edge * edge
    if axis == 0:
        return ref[pl.ds(base + upper * (edge * area - area), area), :]
    if axis == 1:
        return jnp.concatenate(
            [ref[pl.ds(base + row * area + upper * (area - edge), edge), :] for row in range(edge)]
        )
    return ref[pl.ds(base + upper * (edge - 1), area, stride=edge), :]


def write_face(ref, base, edge, axis, upper, value):
    area = edge * edge
    if axis == 0:
        ref[pl.ds(base + upper * (edge * area - area), area), :] = value
    elif axis == 1:
        for row in range(edge):
            ref[pl.ds(base + row * area + upper * (area - edge), edge), :] = value[
                row * edge : row * edge + edge
            ]
    else:
        ref[pl.ds(base + upper * (edge - 1), area, stride=edge), :] = value


def sent_face(ref, send_ref, edge, axis):
    face = jnp.bitwise_and(send_ref[0, axis], 31)
    brick = lax.div(face, 6)
    upper = lax.rem(face, 2)
    return face_value(ref, pl.multiple_of(brick * edge**3, edge**3), edge, axis, upper)


def write_tap(out, field, source_ref, edge, side):
    volume = edge**3
    total = BRICKS * volume
    axis, upper = side // 2, side % 2
    step = edge ** (2 - axis)
    if upper:
        out[pl.ds(0, total - step), :] = field[pl.ds(step, total - step), :]
    else:
        out[pl.ds(step, total - step), :] = field[pl.ds(0, total - step), :]
    for brick in range(BRICKS):
        source = source_ref[0, brick, side]
        near = lax.div(jnp.minimum(source, LOCAL - 1), 6)
        slab = face_value(field, pl.multiple_of(near * volume, volume), edge, axis, 1 - upper)
        rim = jnp.where(source < LOCAL, slab, jnp.zeros_like(slab))
        write_face(out, brick * volume, edge, axis, upper, rim)


def far_rims(info_ref, edge, received):
    volume = edge**3
    for axis in range(3):
        info = info_ref[0, axis]
        face = jnp.bitwise_and(info, 31)
        base = pl.multiple_of(lax.div(face, 6) * volume, volume)
        rim = received[axis][...]
        yield axis, lax.rem(face, 2), base, jnp.where(info >= 32, rim, jnp.zeros_like(rim))


def add_face(ref, base, edge, axis, upper, value):
    write_face(ref, base, edge, axis, upper, face_value(ref, base, edge, axis, upper) + value)


def sigmoid(value):
    return 1.0 / (1.0 + jnp.exp(-value))


def feature_faces(
    features, sides, sources, field, source_out, info_out, face_0, face_1, face_2,
    send_ref, source_ref, brick_ref, sem,
):
    copies = begin(
        sem, (sides, send_ref), (features, field), (sources, source_out), (sources, source_ref)
    )
    for copy in copies:
        copy.wait()
    place = lax.broadcasted_iota(jnp.int32, (1, C1), 1)
    infos = jnp.zeros((1, C1), jnp.int32)
    for axis, out in enumerate((face_0, face_1, face_2)):
        face = send_ref[0, axis]
        brick = lax.div(face, 6)
        linked = source_ref[0, brick, lax.rem(face, 6)] == LOCAL + axis
        infos = jnp.where(place == axis, face + jnp.where(linked, 32, 0), infos)
        base = pl.multiple_of(brick * 512, 512)
        brick_ref[axis] = field[pl.ds(base, 512), :].astype(F32)
        out[...] = face_value(brick_ref.at[axis], 0, 8, axis, lax.rem(face, 2)).astype(BF16)
    info_out[...] = infos


def ready_one(
    source_ref, field_near, conv, down_far, taps, pre, weight, down, field, shifted, sem
):
    copies = begin(sem, (conv, weight), (down_far, down))
    field[...] = field_near[...].astype(F32)
    taps[:, 0:C1] = field_near[...]
    for side in range(6):
        tap = shifted.at[side]
        write_tap(tap, field, source_ref, 8, side)
        taps[:, C1 * (side + 1) : C1 * (side + 2)] = tap[...].astype(BF16)
    copies[0].wait()
    for brick in range(BRICKS):
        rows = pl.ds(512 * brick, 512)
        pre[rows, :] = jnp.dot(taps[rows, :], weight[...], preferred_element_type=F32)
    copies[1].wait()


def level_one(
    info_ref, field, got_0, got_1, got_2, weight, down, pre_near, conv_next, cot_far,
    slope, patches, coarse, face_0, face_1, face_2, weight_next, cotangent,
    pre, hidden, cells, sem,
):
    copies = begin(sem, (conv_next, weight_next), (cot_far, cotangent))
    pre[...] = pre_near[...]
    for axis, upper, base, rim in far_rims(info_ref, 8, (got_0, got_1, got_2)):
        rows = pl.ds(pl.multiple_of(C1 * (2 * axis + upper + 1), C1), C1)
        add = jnp.dot(rim, weight[rows, :], preferred_element_type=F32)
        add_face(pre, base, 8, axis, upper, add)
    for brick in range(BRICKS):
        rows = pl.ds(512 * brick, 512)
        value = pre[rows, :]
        gate = sigmoid(value)
        slope[rows, :] = gate * (1.0 + value * (1.0 - gate))
        hidden[rows, :] = field[rows, :].astype(F32) + value * gate
    low = lax.broadcasted_iota(jnp.int32, (1, 8, C1), 1) < 4
    for r in range(2):
        rows = hidden[pl.ds(r, 1024, stride=2), :].reshape(BRICKS * 4, 2, 2, 2, 8, C1)
        for a in range(2):
            left = rows[:, a, :, 0].reshape(32, 8, C1)
            right = rows[:, a, :, 1].reshape(32, 8, C1)
            first = jnp.where(low, left, pltpu.roll(right, 4, 1))
            second = jnp.where(low, pltpu.roll(left, 4, 1), right)
            for q, value in enumerate((first, second)):
                lane = ((a * 2 + q) * 2 + r) * C1
                patches[:, lane : lane + C1] = value.reshape(256, C1).astype(BF16)
    low_res = jnp.dot(patches[...], down[...], preferred_element_type=F32).astype(BF16)
    coarse[...] = low_res
    send_faces_of(low_res, info_ref, cells, (face_0, face_1, face_2))
    for copy in copies:
        copy.wait()


def split(value, cells):
    cells[0] = value[:, :C1].astype(F32)
    cells[1] = value[:, C1:].astype(F32)


def send_faces_of(value, send_ref, cells, outs):
    split(value, cells)
    for axis, out in enumerate(outs):
        for part in range(2):
            out[:, C1 * part : C1 * part + C1] = sent_face(
                cells.at[part], send_ref, 4, axis
            ).astype(BF16)


def add_cells(ref, base, axis, upper, value):
    for part in range(2):
        add_face(ref.at[part], base, 4, axis, upper, value[:, C1 * part : C1 * part + C1])


def level_two_taps(source_ref, cells, shifted, taps):
    for side in range(6):
        for part in range(2):
            tap = shifted.at[side, part]
            write_tap(tap, cells.at[part], source_ref, 4, side)
            start = C2 * (side + 1) + C1 * part
            taps[:, start : start + C1] = tap[...].astype(BF16)


def ready_two(source_ref, coarse, weight, taps, pre, cells, shifted):
    low_res = coarse[...]
    split(low_res, cells)
    taps[:, 0:C2] = low_res
    level_two_taps(source_ref, cells, shifted, taps)
    split(jnp.dot(taps[...], weight[...], preferred_element_type=F32), pre)


def level_two(
    info_ref, got_0, got_1, got_2, weight, cotangent, pre_near,
    pre, delta, face_0, face_1, face_2,
    cells,
):
    pre[...] = pre_near[...]
    for axis, upper, base, rim in far_rims(info_ref, 4, (got_0, got_1, got_2)):
        rows = pl.ds(pl.multiple_of(C2 * (2 * axis + upper + 1), C2), C2)
        add = jnp.dot(rim, weight[rows, :], preferred_element_type=F32)
        add_cells(pre, base, axis, upper, add)
    value = jnp.concatenate([pre[0], pre[1]], axis=1)
    gate = sigmoid(value)
    change = (cotangent[...].astype(F32) * (gate * (1.0 + value * (1.0 - gate)))).astype(BF16)
    delta[...] = change
    send_faces_of(change, info_ref, cells, (face_0, face_1, face_2))


def core_index():
    return lax.rem(lax.axis_index("scene"), 2)


def ready_back(
    source_ref, info_ref, delta, weight, cotangent, coarse, pre, taps_two, got_0, got_1, got_2,
    kept, sent, encoded, total,
    cells, shifted, taps, both,
):
    change = delta[...]
    split(change, cells)
    taps[:, 0:C2] = change
    level_two_taps(source_ref, cells, shifted, taps)
    value = cotangent[...].astype(F32)
    for tap in range(7):
        lane = C2 * OPPOSITE[tap]
        value = value + nt_dot(taps[:, lane : lane + C2], weight[pl.ds(C2 * tap, C2), :])
    split(value, total)
    value = jnp.concatenate([pre[0], pre[1]], axis=1)
    encoded[...] = (coarse[...].astype(F32) + value * sigmoid(value)).astype(BF16)
    for tap in range(7):
        grad = tn_dot(taps_two[:, C2 * tap : C2 * tap + C2], change)
        rows = pl.ds(C2 * tap, C2)
        both[0, rows, :] = grad[:, :C1]
        both[1, rows, :] = grad[:, C1:]
    for axis, upper, base, rim in far_rims(info_ref, 4, (got_0, got_1, got_2)):
        rows = pl.ds(pl.multiple_of(C2 * (2 * axis + upper + 1), C2), C2)
        for part in range(2):
            here = face_value(cells.at[part], base, 4, axis, upper).astype(BF16)
            both[part, rows, :] = both[part, rows, :] + tn_dot(rim, here)
    core = core_index()
    kept[...] = both[core]
    sent[...] = both[1 - core].astype(BF16)


def backward(
    info_ref, got_0, got_1, got_2, rim_0, rim_1, rim_2, weight, down, patches, slope,
    taps_one, total_near, kept, sent,
    total, patch_grad, spread, delta_one, both,
):
    total[...] = total_near[...]
    for axis, upper, base, rim in far_rims(info_ref, 4, (got_0, got_1, got_2)):
        rows = pl.ds(pl.multiple_of(C2 * (2 * axis + 2 - upper), C2), C2)
        add_cells(total, base, axis, upper, nt_dot(rim, weight[rows, :]))
    upstream = jnp.concatenate([total[0], total[1]], axis=1).astype(BF16)
    grad_down = tn_dot(patches[...], upstream)
    both[0, pl.ds(ONE_ROWS, DOWN_ROWS), :] = grad_down[:, :C1]
    both[1, pl.ds(ONE_ROWS, DOWN_ROWS), :] = grad_down[:, C1:]
    patch_grad[...] = nt_dot(upstream, down[...])
    low = lax.broadcasted_iota(jnp.int32, (1, 8, C1), 1) < 4
    for r in range(2):
        halves = []
        for a in range(2):
            lane = (a * 4 + r) * C1
            first = patch_grad[:, lane : lane + C1].reshape(32, 8, C1)
            lane = lane + 2 * C1
            second = patch_grad[:, lane : lane + C1].reshape(32, 8, C1)
            left = jnp.where(low, first, pltpu.roll(second, 4, 1))
            right = jnp.where(low, pltpu.roll(first, 4, 1), second)
            halves.append(jnp.stack([left, right], axis=1).reshape(BRICKS * 4, 4, 8, C1))
        spread[pl.ds(r, 1024, stride=2), :] = jnp.stack(halves, axis=1).reshape(1024, C1)
    change = (spread[...] * slope[...]).astype(BF16)
    delta_one[...] = change
    spread[...] = change.astype(F32)
    grad_one = tn_dot(delta_one[...], taps_one[...])
    for tap in range(7):
        block = grad_one[:, C1 * tap : C1 * tap + C1].T
        for start in range(0, C1, 64):
            row = C1 * tap + start
            both[row // ONE_ROWS, pl.ds(row % ONE_ROWS, 64), :] = block[start : start + 64]
    for axis, upper, base, rim in far_rims(info_ref, 8, (rim_0, rim_1, rim_2)):
        add = tn_dot(rim, face_value(spread, base, 8, axis, upper).astype(BF16))
        for start in range(0, C1, 64):
            row = C1 * (2 * axis + upper + 1) + start
            half = lax.div(row, ONE_ROWS)
            rows = pl.ds(pl.multiple_of(row - half * ONE_ROWS, 64), 64)
            both[half, rows, :] = both[half, rows, :] + add[start : start + 64]
    core = core_index()
    kept[...] = both[core]
    sent[...] = both[1 - core].astype(BF16)


def pair_sum(kept_a, got_a, kept_b, got_b, out):
    out[pl.ds(0, EARLY), :] = (kept_a[...] + got_a[...].astype(F32)).astype(BF16)
    out[pl.ds(EARLY, TWO_ROWS), :] = (kept_b[...] + got_b[...].astype(F32)).astype(BF16)
    out[pl.ds(HALF, PLANE * CHUNK - HALF), :] = jnp.zeros((PLANE * CHUNK - HALF, C1), BF16)


def group_sum(parts, out):
    total = parts[0].astype(F32)
    for index in range(1, parts.shape[0]):
        total = total + parts[index].astype(F32)
    total = total.astype(BF16)
    for index in range(out.shape[0]):
        out[index] = total


def unpack(turned, source, *refs):
    one, down, two, stage, sem = refs[-5:]
    half = core_index()
    if turned:
        half = 1 - half
    lanes = pl.ds(pl.multiple_of(half * C1, C1), C1)
    targets = (
        (EARLY, TWO_ROWS, two.at[:, lanes]),
        (ONE_ROWS, DOWN_ROWS, down.at[:, lanes]),
        (0, ONE_ROWS, one.at[pl.ds(pl.multiple_of(half * ONE_ROWS, ONE_ROWS), ONE_ROWS), :]),
    )
    copies = []
    for index, (start, size, target) in enumerate(targets):
        rows = pl.ds(start, size)
        stage[rows, :] = source[rows, :].astype(F32)
        copies.append(pltpu.make_async_copy(stage.at[rows, :], target, sem.at[index]))
        copies[-1].start()
    for copy in copies:
        copy.wait()


def swapped(value, axis, bit):
    mask = 2**bit
    pairs = [(source, source ^ mask) for source in range(lax.axis_size(axis))]
    return lax.ppermute(value, axis, pairs)


def exchanged(faces):
    got = []
    for bit, face in enumerate(faces):
        got.append(swapped(face, "kd", bit))
    return got


def step(features, send_faces, face_source, cotangent, conv_one, down_weight, conv_two):
    sides = send_faces.reshape(1, 3)
    weight_one = conv_one.reshape(7 * C1, C1)
    weight_two = conv_two.reshape(7 * C2, C2)
    dma = pltpu.SemaphoreType.DMA
    field, sources, info, *sent = call(
        feature_faces,
        [(hbm, features.reshape(2048, C1)), (hbm, sides), (hbm, face_source)],
        [(vmem, (2048, C1), BF16), (vmem, (1, BRICKS, 6), jnp.int32)]
        + [(vmem, (1, C1), jnp.int32)]
        + [(vmem, (64, C1), BF16)] * 3,
        [
            pltpu.SMEM((1, 3), jnp.int32),
            pltpu.SMEM((1, BRICKS, 6), jnp.int32),
            pltpu.VMEM((3, 512, C1), F32),
            dma((4,)),
        ],
    )
    got_field = [(vmem, face) for face in exchanged(sent)]
    taps_one, pre_one, near_one, down = call(
        ready_one,
        [(smem, sources), (vmem, field)]
        + [(hbm, weight_one), (hbm, down_weight)],
        [
            (vmem, (2048, 7 * C1), BF16),
            (vmem, (2048, C1), F32),
            (vmem, (7 * C1, C1), BF16),
            (vmem, (8 * C1, C2), BF16),
        ],
        [pltpu.VMEM((2048, C1), F32), pltpu.VMEM((6, 2048, C1), F32), dma((2,))],
    )
    slope, patches, coarse, face_0, face_1, face_2, weight, upstream = call(
        level_one,
        [(smem, info), (vmem, field)]
        + got_field
        + [(vmem, near_one), (vmem, down), (vmem, pre_one)]
        + [(hbm, weight_two), (hbm, cotangent.reshape(256, C2))],
        [(vmem, (2048, C1), F32), (vmem, (256, 8 * C1), BF16), (vmem, (256, C2), BF16)]
        + [(vmem, (16, C2), BF16)] * 3
        + [(vmem, (7 * C2, C2), BF16), (vmem, (256, C2), BF16)],
        [
            pltpu.VMEM((2048, C1), F32),
            pltpu.VMEM((2048, C1), F32),
            pltpu.VMEM((2, 256, C1), F32),
            dma((2,)),
        ],
    )
    got_coarse = [(vmem, face) for face in exchanged((face_0, face_1, face_2))]
    taps_two, pre_two = call(
        ready_two,
        [(smem, sources), (vmem, coarse), (vmem, weight)],
        [(vmem, (256, 7 * C2), BF16), (vmem, (2, 256, C1), F32)],
        [pltpu.VMEM((2, 256, C1), F32), pltpu.VMEM((6, 2, 256, C1), F32)],
    )
    pre_two, delta, *sent = call(
        level_two,
        [(smem, info)]
        + got_coarse
        + [(vmem, weight), (vmem, upstream), (vmem, pre_two)],
        [(vmem, (2, 256, C1), F32), (vmem, (256, C2), BF16)] + [(vmem, (16, C2), BF16)] * 3,
        [pltpu.VMEM((2, 256, C1), F32)],
    )
    got = [(vmem, face) for face in exchanged(sent)]
    kept_two, sent_two, encoded, total = call(
        ready_back,
        [(smem, sources), (smem, info), (vmem, delta), (vmem, weight), (vmem, upstream)]
        + [(vmem, coarse), (vmem, pre_two), (vmem, taps_two)]
        + got_coarse,
        [(vmem, (TWO_ROWS, C1), F32), (vmem, (TWO_ROWS, C1), BF16), (vmem, (256, C2), BF16)]
        + [(vmem, (2, 256, C1), F32)],
        [
            pltpu.VMEM((2, 256, C1), F32),
            pltpu.VMEM((6, 2, 256, C1), F32),
            pltpu.VMEM((256, 7 * C2), BF16),
            pltpu.VMEM((2, TWO_ROWS, C1), F32),
        ],
    )
    got_two = swapped(sent_two, "scene", 0)
    kept, sent = call(
        backward,
        [(smem, info)]
        + got
        + got_field
        + [(vmem, weight), (vmem, down), (vmem, patches), (vmem, slope), (vmem, taps_one)]
        + [(vmem, total)],
        [(vmem, (EARLY, C1), F32), (vmem, (EARLY, C1), BF16)],
        [
            pltpu.VMEM((2, 256, C1), F32),
            pltpu.VMEM((256, 8 * C1), F32),
            pltpu.VMEM((2048, C1), F32),
            pltpu.VMEM((2048, C1), BF16),
            pltpu.VMEM((2, EARLY, C1), F32),
        ],
    )
    got = swapped(sent, "scene", 0)
    groups = [[2 * chip + core for chip in range(PLANE)] for core in range(2)]
    (packed,) = call(
        pair_sum,
        [(vmem, kept), (vmem, got), (vmem, kept_two), (vmem, got_two)],
        [(vmem, (PLANE * CHUNK, C1), BF16)],
    )
    parts = lax.all_to_all(
        packed.reshape(PLANE, CHUNK, C1), "scene", 0, 0, axis_index_groups=groups
    )
    (copies,) = call(group_sum, [(vmem, parts)], [(vmem, (DEPTH, CHUNK, C1), BF16)])
    parts = lax.all_to_all(copies, "kd", 0, 0)
    (copies,) = call(group_sum, [(vmem, parts)], [(vmem, (PLANE, CHUNK, C1), BF16)])
    own = lax.all_to_all(copies, "scene", 0, 0, axis_index_groups=groups)
    own = own.reshape(PLANE * CHUNK, C1)
    other = swapped(own, "scene", 0)
    shapes = [(hbm, (7 * C1, C1), F32), (hbm, (8 * C1, C2), F32), (hbm, (7 * C2, C2), F32)]
    scratch = [pltpu.VMEM((HALF, C1), F32), dma((3,))]
    partial = call(functools.partial(unpack, False), [(vmem, own)], shapes, scratch)
    one, low, two = call(
        functools.partial(unpack, True),
        [(vmem, other)] + [(hbm, value) for value in partial],
        shapes,
        scratch,
        {1: 0, 2: 1, 3: 2},
    )
    return (
        encoded.reshape(1, BRICKS, 64, C2),
        one.reshape(7, C1, C1),
        low,
        two.reshape(7, C2, C2),
    )


def solution(mesh):
    placed = (
        P("scene", "kd", None, None),
        P("scene", "kd", None, None),
        P("scene", "kd", None),
        P("scene", "kd", None, None),
        P(),
        P(),
        P(),
    )
    return jax.shard_map(
        step,
        mesh=mesh,
        in_specs=placed,
        out_specs=(P("scene", "kd", None, None), P(), P(), P()),
        check_vma=False,
    )
```

```python
import functools

import jax
import jax.numpy as jnp
from jax import lax
from jax.experimental import pallas as pl
from jax.experimental.pallas import tpu as pltpu
from jax.sharding import PartitionSpec as P


OPPOSITE = (0, 2, 1, 4, 3, 6, 5)
BRICKS = 4
C1 = 128
C2 = 256
LOCAL = 6 * BRICKS
PLANE = 16
DEPTH = 8
STEPS = (3, 2, 1)
CHUNK = 208
ONE_ROWS = 448
DOWN_ROWS = 1024
TWO_ROWS = 1792
EARLY = ONE_ROWS + DOWN_ROWS
HALF = EARLY + TWO_ROWS
F32 = jnp.float32
BF16 = jnp.bfloat16


def vmem():
    return pl.BlockSpec(memory_space=pltpu.VMEM)


def smem():
    return pl.BlockSpec(memory_space=pltpu.SMEM)


def hbm():
    return pl.BlockSpec(memory_space=pltpu.HBM)


LIMIT = 24 * 1024 * 1024


def far(value):
    return pltpu.with_memory_space_constraint(value, pltpu.HBM)


def call(body, inputs, outs, scratch=(), aliases=None):
    return pl.pallas_call(
        body,
        out_shape=[jax.ShapeDtypeStruct(shape, dtype) for _, shape, dtype in outs],
        in_specs=[place() for place, _ in inputs],
        out_specs=[place() for place, _, _ in outs],
        scratch_shapes=list(scratch),
        input_output_aliases=aliases or {},
        compiler_params=pltpu.CompilerParams(vmem_limit_bytes=LIMIT),
    )(*[far(value) if place is hbm else value for place, value in inputs])


def begin(sem, *pairs):
    copies = [
        pltpu.make_async_copy(source, target, sem.at[index])
        for index, (source, target) in enumerate(pairs)
    ]
    for copy in copies:
        copy.start()
    return copies


def nt_dot(left, right):
    return lax.dot_general(left, right, (((1,), (1,)), ((), ())), preferred_element_type=F32)


def tn_dot(left, right):
    return lax.dot_general(left, right, (((0,), (0,)), ((), ())), preferred_element_type=F32)


def face_value(ref, base, edge, axis, upper):
    area = edge * edge
    if axis == 0:
        return ref[pl.ds(base + upper * (edge * area - area), area), :]
    if axis == 1:
        return jnp.concatenate(
            [ref[pl.ds(base + row * area + upper * (area - edge), edge), :] for row in range(edge)]
        )
    return ref[pl.ds(base + upper * (edge - 1), area, stride=edge), :]


def write_face(ref, base, edge, axis, upper, value):
    area = edge * edge
    if axis == 0:
        ref[pl.ds(base + upper * (edge * area - area), area), :] = value
    elif axis == 1:
        for row in range(edge):
            ref[pl.ds(base + row * area + upper * (area - edge), edge), :] = value[
                row * edge : row * edge + edge
            ]
    else:
        ref[pl.ds(base + upper * (edge - 1), area, stride=edge), :] = value


def sent_face(ref, send_ref, edge, axis):
    face = jnp.bitwise_and(send_ref[0, axis], 31)
    brick = lax.div(face, 6)
    upper = lax.rem(face, 2)
    return face_value(ref, pl.multiple_of(brick * edge**3, edge**3), edge, axis, upper)


def local_rim(field, source_ref, edge, side, brick):
    volume = edge**3
    source = source_ref[0, brick, side]
    near = lax.div(jnp.minimum(source, LOCAL - 1), 6)
    base = pl.multiple_of(near * volume, volume)
    slab = face_value(field, base, edge, side // 2, 1 - side % 2)
    return jnp.where(source < LOCAL, slab, jnp.zeros_like(slab))


def write_tap(out, field, source_ref, edge, side):
    volume = edge**3
    total = BRICKS * volume
    axis, upper = side // 2, side % 2
    step = edge ** (2 - axis)
    if upper:
        out[pl.ds(0, total - step), :] = field[pl.ds(step, total - step), :]
    else:
        out[pl.ds(step, total - step), :] = field[pl.ds(0, total - step), :]
    for brick in range(BRICKS):
        rim = local_rim(field, source_ref, edge, side, brick)
        write_face(out, brick * volume, edge, axis, upper, rim)


def far_rims(info_ref, edge, received):
    volume = edge**3
    for axis in range(3):
        info = info_ref[0, axis]
        face = jnp.bitwise_and(info, 31)
        base = pl.multiple_of(lax.div(face, 6) * volume, volume)
        rim = received[axis][...]
        yield axis, lax.rem(face, 2), base, jnp.where(info >= 32, rim, jnp.zeros_like(rim))


def add_face(ref, base, edge, axis, upper, value):
    write_face(ref, base, edge, axis, upper, face_value(ref, base, edge, axis, upper) + value)


def sigmoid(value):
    return 0.5 * jnp.tanh(0.5 * value) + 0.5


def feature_faces(
    features, sides, sources, field, source_out, info_out, face_0, face_1, face_2,
    send_ref, source_ref, brick_ref, sem,
):
    copies = begin(
        sem, (sides, send_ref), (features, field), (sources, source_out), (sources, source_ref)
    )
    for copy in copies:
        copy.wait()
    place = lax.broadcasted_iota(jnp.int32, (1, C1), 1)
    infos = jnp.zeros((1, C1), jnp.int32)
    for axis, out in enumerate((face_0, face_1, face_2)):
        face = send_ref[0, axis]
        brick = lax.div(face, 6)
        linked = source_ref[0, brick, lax.rem(face, 6)] == LOCAL + axis
        infos = jnp.where(place == axis, face + jnp.where(linked, 32, 0), infos)
        base = pl.multiple_of(brick * 512, 512)
        brick_ref[axis] = field[pl.ds(base, 512), :].astype(F32)
        out[...] = face_value(brick_ref.at[axis], 0, 8, axis, lax.rem(face, 2)).astype(BF16)
    info_out[...] = infos


def ready_one(
    source_ref, field_near, conv, down_far, taps, pre, weight, down, field, shifted, sem
):
    copies = begin(sem, (conv, weight), (down_far, down))
    field[...] = field_near[...].astype(F32)
    taps[:, 0:C1] = field_near[...]
    for side in range(6):
        lanes = slice(C1 * (side + 1), C1 * (side + 2))
        upper = side % 2
        if side < 2:
            to, start = (0, 64) if upper else (64, 0)
            taps[pl.ds(to, 1984), lanes] = field_near[pl.ds(start, 1984), :]
            for brick in range(BRICKS):
                rim = local_rim(field_near, source_ref, 8, side, brick)
                taps[pl.ds(512 * brick + 448 * upper, 64), lanes] = rim
        elif side < 4:
            for brick in range(BRICKS):
                here = field[pl.ds(512 * brick, 512), :].reshape(8, 64, C1)
                rim = local_rim(field, source_ref, 8, side, brick).reshape(8, 8, C1)
                pair = (here[:, 8:], rim) if upper else (rim, here[:, :56])
                tap = jnp.concatenate(pair, axis=1).reshape(512, C1)
                taps[pl.ds(512 * brick, 512), lanes] = tap.astype(BF16)
        else:
            tap = shifted.at[upper]
            write_tap(tap, field, source_ref, 8, side)
            taps[:, lanes] = tap[...].astype(BF16)
    copies[0].wait()
    for brick in range(BRICKS):
        rows = pl.ds(512 * brick, 512)
        pre[rows, :] = jnp.dot(taps[rows, :], weight[...], preferred_element_type=F32)
    copies[1].wait()


def level_one(
    info_ref, field, got_0, got_1, got_2, weight, down, pre_near, conv_next, cot_far,
    pre, patches, coarse, face_0, face_1, face_2, weight_next, cotangent,
    hidden, cells, sem,
):
    copies = begin(sem, (conv_next, weight_next), (cot_far, cotangent))
    pre[...] = pre_near[...]
    for axis, upper, base, rim in far_rims(info_ref, 8, (got_0, got_1, got_2)):
        rows = pl.ds(pl.multiple_of(C1 * (2 * axis + upper + 1), C1), C1)
        add = jnp.dot(rim, weight[rows, :], preferred_element_type=F32)
        add_face(pre, base, 8, axis, upper, add)
    for brick in range(BRICKS):
        rows = pl.ds(512 * brick, 512)
        value = pre[rows, :]
        hidden[rows, :] = field[rows, :].astype(F32) + value * sigmoid(value)
    low = lax.broadcasted_iota(jnp.int32, (1, 8, C1), 1) < 4
    for r in range(2):
        rows = hidden[pl.ds(r, 1024, stride=2), :].reshape(BRICKS * 4, 2, 2, 2, 8, C1)
        for a in range(2):
            left = rows[:, a, :, 0].reshape(32, 8, C1)
            right = rows[:, a, :, 1].reshape(32, 8, C1)
            first = jnp.where(low, left, pltpu.roll(right, 4, 1))
            second = jnp.where(low, pltpu.roll(left, 4, 1), right)
            for q, value in enumerate((first, second)):
                lane = ((a * 2 + q) * 2 + r) * C1
                patches[:, lane : lane + C1] = value.reshape(256, C1).astype(BF16)
    low_res = jnp.dot(patches[...], down[...], preferred_element_type=F32).astype(BF16)
    coarse[...] = low_res
    send_faces_of(low_res, info_ref, cells, (face_0, face_1, face_2))
    for copy in copies:
        copy.wait()


def split(value, cells):
    cells[0] = value[:, :C1].astype(F32)
    cells[1] = value[:, C1:].astype(F32)


def send_faces_of(value, send_ref, cells, outs):
    split(value, cells)
    for axis, out in enumerate(outs):
        for part in range(2):
            out[:, C1 * part : C1 * part + C1] = sent_face(
                cells.at[part], send_ref, 4, axis
            ).astype(BF16)


def add_cells(ref, base, axis, upper, value):
    for part in range(2):
        add_face(ref.at[part], base, 4, axis, upper, value[:, C1 * part : C1 * part + C1])


def level_two_taps(source_ref, cells, shifted, taps):
    for side in range(6):
        for part in range(2):
            tap = shifted.at[side, part]
            write_tap(tap, cells.at[part], source_ref, 4, side)
            start = C2 * (side + 1) + C1 * part
            taps[:, start : start + C1] = tap[...].astype(BF16)


def ready_two(source_ref, coarse, weight, pre_one, taps, pre, slope, cells, shifted):
    low_res = coarse[...]
    split(low_res, cells)
    taps[:, 0:C2] = low_res
    level_two_taps(source_ref, cells, shifted, taps)
    split(jnp.dot(taps[...], weight[...], preferred_element_type=F32), pre)
    for brick in range(BRICKS):
        rows = pl.ds(512 * brick, 512)
        value = pre_one[rows, :]
        gate = sigmoid(value)
        slope[rows, :] = gate * (1.0 + value * (1.0 - gate))


def level_two(
    info_ref, got_0, got_1, got_2, weight, cotangent, pre_near,
    pre, delta, face_0, face_1, face_2,
    cells,
):
    pre[...] = pre_near[...]
    for axis, upper, base, rim in far_rims(info_ref, 4, (got_0, got_1, got_2)):
        rows = pl.ds(pl.multiple_of(C2 * (2 * axis + upper + 1), C2), C2)
        add = jnp.dot(rim, weight[rows, :], preferred_element_type=F32)
        add_cells(pre, base, axis, upper, add)
    value = jnp.concatenate([pre[0], pre[1]], axis=1)
    gate = sigmoid(value)
    change = (cotangent[...].astype(F32) * (gate * (1.0 + value * (1.0 - gate)))).astype(BF16)
    delta[...] = change
    send_faces_of(change, info_ref, cells, (face_0, face_1, face_2))


def core_index():
    return lax.rem(lax.axis_index("scene"), 2)


def ready_back(
    source_ref, info_ref, delta, weight, cotangent, coarse, pre, taps_two, got_0, got_1, got_2,
    kept, sent, encoded, total,
    cells, shifted, taps,
):
    change = delta[...]
    split(change, cells)
    taps[:, 0:C2] = change
    level_two_taps(source_ref, cells, shifted, taps)
    value = cotangent[...].astype(F32)
    for tap in range(7):
        lane = C2 * OPPOSITE[tap]
        value = value + nt_dot(taps[:, lane : lane + C2], weight[pl.ds(C2 * tap, C2), :])
    split(value, total)
    value = jnp.concatenate([pre[0], pre[1]], axis=1)
    encoded[...] = (coarse[...].astype(F32) + value * sigmoid(value)).astype(BF16)
    far = {}
    for axis, upper, base, rim in far_rims(info_ref, 4, (got_0, got_1, got_2)):
        here = [face_value(cells.at[part], base, 4, axis, upper) for part in range(2)]
        add = tn_dot(rim, jnp.concatenate(here, axis=1).astype(BF16))
        for side in range(2):
            far[2 * axis + side + 1] = jnp.where(upper == side, add, jnp.zeros_like(add))
    first = core_index() == 0
    for tap in range(7):
        grad = tn_dot(taps_two[:, C2 * tap : C2 * tap + C2], change)
        if tap:
            grad = grad + far[tap]
        keep_half(first, grad, kept, sent, pl.ds(C2 * tap, C2))


def keep_half(first, grad, kept, sent, rows):
    low, high = grad[:, :C1], grad[:, C1:]
    kept[rows, :] = jnp.where(first, low, high)
    sent[rows, :] = jnp.where(first, high, low).astype(BF16)


def backward(
    info_ref, got_0, got_1, got_2, rim_0, rim_1, rim_2, weight, down, patches, slope,
    taps_one, total_near, sent_two, kept, sent,
    total, patch_grad, spread, delta_one, both,
):
    total[...] = total_near[...]
    for axis, upper, base, rim in far_rims(info_ref, 4, (got_0, got_1, got_2)):
        rows = pl.ds(pl.multiple_of(C2 * (2 * axis + 2 - upper), C2), C2)
        add_cells(total, base, axis, upper, nt_dot(rim, weight[rows, :]))
    upstream = jnp.concatenate([total[0], total[1]], axis=1).astype(BF16)
    core = core_index()
    for start in range(0, DOWN_ROWS, C2):
        grad = tn_dot(patches[:, start : start + C2], upstream)
        keep_half(core == 0, grad, kept, sent, pl.ds(ONE_ROWS + start, C2))
    sent[pl.ds(EARLY, TWO_ROWS), :] = sent_two[...]
    patch_grad[...] = nt_dot(upstream, down[...])
    low = lax.broadcasted_iota(jnp.int32, (1, 8, C1), 1) < 4
    for r in range(2):
        halves = []
        for a in range(2):
            lane = (a * 4 + r) * C1
            first = patch_grad[:, lane : lane + C1].reshape(32, 8, C1)
            lane = lane + 2 * C1
            second = patch_grad[:, lane : lane + C1].reshape(32, 8, C1)
            left = jnp.where(low, first, pltpu.roll(second, 4, 1))
            right = jnp.where(low, pltpu.roll(first, 4, 1), second)
            halves.append(jnp.stack([left, right], axis=1).reshape(BRICKS * 4, 4, 8, C1))
        spread[pl.ds(r, 1024, stride=2), :] = jnp.stack(halves, axis=1).reshape(1024, C1)
    change = (spread[...] * slope[...]).astype(BF16)
    delta_one[...] = change
    spread[...] = change.astype(F32)
    grad_one = tn_dot(delta_one[...], taps_one[...])
    for tap in range(7):
        block = grad_one[:, C1 * tap : C1 * tap + C1].T
        for start in range(0, C1, 64):
            row = C1 * tap + start
            both[row // ONE_ROWS, pl.ds(row % ONE_ROWS, 64), :] = block[start : start + 64]
    for axis, upper, base, rim in far_rims(info_ref, 8, (rim_0, rim_1, rim_2)):
        add = tn_dot(rim, face_value(spread, base, 8, axis, upper).astype(BF16))
        for start in range(0, C1, 64):
            row = C1 * (2 * axis + upper + 1) + start
            half = lax.div(row, ONE_ROWS)
            rows = pl.ds(pl.multiple_of(row - half * ONE_ROWS, 64), 64)
            both[half, rows, :] = both[half, rows, :] + add[start : start + 64]
    kept[pl.ds(0, ONE_ROWS), :] = both[core]
    sent[pl.ds(0, ONE_ROWS), :] = both[1 - core].astype(BF16)


def pair_sum(kept_a, kept_b, got, out):
    early, late = pl.ds(0, EARLY), pl.ds(EARLY, TWO_ROWS)
    out[early, :] = (kept_a[...] + got[early, :].astype(F32)).astype(BF16)
    out[late, :] = (kept_b[...] + got[late, :].astype(F32)).astype(BF16)
    out[pl.ds(HALF, PLANE * CHUNK - HALF), :] = jnp.zeros((PLANE * CHUNK - HALF, C1), BF16)


def group_sum(parts, out):
    total = parts[0].astype(F32)
    for index in range(1, parts.shape[0]):
        total = total + parts[index].astype(F32)
    total = total.astype(BF16)
    for index in range(out.shape[0]):
        out[index] = total


def depth_pair(own, got, out):
    out[...] = (own[...].astype(F32) + got[...].astype(F32)).astype(BF16)


def depth_sum(own, got_3, got_2, got_1, out, parts):
    here = lax.axis_index("kd")
    pair, odd = lax.div(here, 2), lax.rem(here, 2)
    parts[pair] = own[0]
    parts[lax.rem(pair + 2, 4)] = got_3[0]
    parts[lax.rem(pair + 1 + 2 * odd, 4)] = got_2[0]
    parts[lax.rem(pair + 3 - 2 * odd, 4)] = got_1[0]
    group_sum(parts, out)


def unpack(turned, source, *refs):
    one, down, two, stage, sem = refs[-5:]
    half = core_index()
    if turned:
        half = 1 - half
    lanes = pl.ds(pl.multiple_of(half * C1, C1), C1)
    place = pl.multiple_of(half * ONE_ROWS, ONE_ROWS)
    targets = [
        (EARLY + row, 448, two.at[pl.ds(row, 448), lanes]) for row in range(0, TWO_ROWS, 448)
    ]
    targets += [
        (ONE_ROWS + row, 512, down.at[pl.ds(row, 512), lanes]) for row in range(0, DOWN_ROWS, 512)
    ]
    targets.append((0, ONE_ROWS, one.at[pl.ds(place, ONE_ROWS), :]))
    copies = []
    for index, (start, size, target) in enumerate(targets):
        rows = pl.ds(start, size)
        stage[rows, :] = source[rows, :].astype(F32)
        copies.append(pltpu.make_async_copy(stage.at[rows, :], target, sem.at[index]))
        copies[-1].start()
    for copy in copies:
        copy.wait()


def swapped(value, axis, bit):
    mask = 2**bit
    pairs = [(source, source ^ mask) for source in range(lax.axis_size(axis))]
    return lax.ppermute(value, axis, pairs)


def exchanged(faces):
    got = []
    for bit, face in enumerate(faces):
        got.append(swapped(face, "kd", bit))
    return got


def step(features, send_faces, face_source, cotangent, conv_one, down_weight, conv_two):
    sides = send_faces.reshape(1, 3)
    weight_one = conv_one.reshape(7 * C1, C1)
    weight_two = conv_two.reshape(7 * C2, C2)
    dma = pltpu.SemaphoreType.DMA
    field, sources, info, *sent = call(
        feature_faces,
        [(hbm, features.reshape(2048, C1)), (hbm, sides), (hbm, face_source)],
        [(vmem, (2048, C1), BF16), (vmem, (1, BRICKS, 6), jnp.int32)]
        + [(vmem, (1, C1), jnp.int32)]
        + [(vmem, (64, C1), BF16)] * 3,
        [
            pltpu.SMEM((1, 3), jnp.int32),
            pltpu.SMEM((1, BRICKS, 6), jnp.int32),
            pltpu.VMEM((3, 512, C1), F32),
            dma((4,)),
        ],
    )
    got_field = [(vmem, face) for face in exchanged(sent)]
    taps_one, pre_one, near_one, down = call(
        ready_one,
        [(smem, sources), (vmem, field)]
        + [(hbm, weight_one), (hbm, down_weight)],
        [
            (vmem, (2048, 7 * C1), BF16),
            (vmem, (2048, C1), F32),
            (vmem, (7 * C1, C1), BF16),
            (vmem, (8 * C1, C2), BF16),
        ],
        [pltpu.VMEM((2048, C1), F32), pltpu.VMEM((2, 2048, C1), F32), dma((2,))],
    )
    pre_one, patches, coarse, face_0, face_1, face_2, weight, upstream = call(
        level_one,
        [(smem, info), (vmem, field)]
        + got_field
        + [(vmem, near_one), (vmem, down), (vmem, pre_one)]
        + [(hbm, weight_two), (hbm, cotangent.reshape(256, C2))],
        [(vmem, (2048, C1), F32), (vmem, (256, 8 * C1), BF16), (vmem, (256, C2), BF16)]
        + [(vmem, (16, C2), BF16)] * 3
        + [(vmem, (7 * C2, C2), BF16), (vmem, (256, C2), BF16)],
        [pltpu.VMEM((2048, C1), F32), pltpu.VMEM((2, 256, C1), F32), dma((2,))],
    )
    got_coarse = [(vmem, face) for face in exchanged((face_0, face_1, face_2))]
    taps_two, pre_two, slope = call(
        ready_two,
        [(smem, sources), (vmem, coarse), (vmem, weight), (vmem, pre_one)],
        [(vmem, (256, 7 * C2), BF16), (vmem, (2, 256, C1), F32), (vmem, (2048, C1), F32)],
        [pltpu.VMEM((2, 256, C1), F32), pltpu.VMEM((6, 2, 256, C1), F32)],
    )
    pre_two, delta, *sent = call(
        level_two,
        [(smem, info)]
        + got_coarse
        + [(vmem, weight), (vmem, upstream), (vmem, pre_two)],
        [(vmem, (2, 256, C1), F32), (vmem, (256, C2), BF16)] + [(vmem, (16, C2), BF16)] * 3,
        [pltpu.VMEM((2, 256, C1), F32)],
    )
    got = [(vmem, face) for face in exchanged(sent)]
    kept_two, sent_two, encoded, total = call(
        ready_back,
        [(smem, sources), (smem, info), (vmem, delta), (vmem, weight), (vmem, upstream)]
        + [(vmem, coarse), (vmem, pre_two), (vmem, taps_two)]
        + got_coarse,
        [(vmem, (TWO_ROWS, C1), F32), (vmem, (TWO_ROWS, C1), BF16), (vmem, (256, C2), BF16)]
        + [(vmem, (2, 256, C1), F32)],
        [
            pltpu.VMEM((2, 256, C1), F32),
            pltpu.VMEM((6, 2, 256, C1), F32),
            pltpu.VMEM((256, 7 * C2), BF16),
        ],
    )
    kept, sent = call(
        backward,
        [(smem, info)]
        + got
        + got_field
        + [(vmem, weight), (vmem, down), (vmem, patches), (vmem, slope), (vmem, taps_one)]
        + [(vmem, total), (vmem, sent_two)],
        [(vmem, (EARLY, C1), F32), (vmem, (HALF, C1), BF16)],
        [
            pltpu.VMEM((2, 256, C1), F32),
            pltpu.VMEM((256, 8 * C1), F32),
            pltpu.VMEM((2048, C1), F32),
            pltpu.VMEM((2048, C1), BF16),
            pltpu.VMEM((2, ONE_ROWS, C1), F32),
        ],
    )
    got = swapped(sent, "scene", 0)
    groups = [[2 * chip + core for chip in range(PLANE)] for core in range(2)]
    (packed,) = call(
        pair_sum, [(vmem, kept), (vmem, kept_two), (vmem, got)], [(vmem, (PLANE * CHUNK, C1), BF16)]
    )
    parts = lax.all_to_all(
        packed.reshape(PLANE, CHUNK, C1), "scene", 0, 0, axis_index_groups=groups
    )
    (piece,) = call(group_sum, [(vmem, parts)], [(vmem, (1, CHUNK, C1), BF16)])
    (piece,) = call(
        depth_pair, [(vmem, piece), (vmem, swapped(piece, "kd", 0))], [(vmem, (1, CHUNK, C1), BF16)]
    )
    pieces = [piece]
    for step in STEPS:
        pairs = [
            (source, (source + (2 * (source % 2) - 1) * step) % DEPTH)
            for source in range(DEPTH)
        ]
        pieces.append(lax.ppermute(piece, "kd", pairs))
    (copies,) = call(
        depth_sum,
        [(vmem, value) for value in pieces],
        [(vmem, (PLANE, CHUNK, C1), BF16)],
        [pltpu.VMEM((4, CHUNK, C1), BF16)],
    )
    own = lax.all_to_all(copies, "scene", 0, 0, axis_index_groups=groups)
    own = own.reshape(PLANE * CHUNK, C1)
    other = swapped(own, "scene", 0)
    shapes = [(hbm, (7 * C1, C1), F32), (hbm, (8 * C1, C2), F32), (hbm, (7 * C2, C2), F32)]
    scratch = [pltpu.VMEM((HALF, C1), F32), dma((7,))]
    partial = call(functools.partial(unpack, False), [(vmem, own)], shapes, scratch)
    one, low, two = call(
        functools.partial(unpack, True),
        [(vmem, other)] + [(hbm, value) for value in partial],
        shapes,
        scratch,
        {1: 0, 2: 1, 3: 2},
    )
    return (
        encoded.reshape(1, BRICKS, 64, C2),
        one.reshape(7, C1, C1),
        low,
        two.reshape(7, C2, C2),
    )


def solution(mesh):
    placed = (
        P("scene", "kd", None, None),
        P("scene", "kd", None, None),
        P("scene", "kd", None),
        P("scene", "kd", None, None),
        P(),
        P(),
        P(),
    )
    return jax.shard_map(
        step,
        mesh=mesh,
        in_specs=placed,
        out_specs=(P("scene", "kd", None, None), P(), P(), P()),
        check_vma=False,
    )
```
